128 devices in a mesh: gx: 8 (over z, core), gy: 16 (over y, x).
Axes of the slice: x: 4, y: 4, z: 4, core: 2. Of those that a mesh axis runs over, the one named last changes fastest.
Arguments:
- offsets: float32 [3, 2097152], P(None, ('gx', 'gy')), may hold values from -5 to 5
- weights: float32 [2097152], P(('gx', 'gy')), may hold values from -1 to 1
- owners: int32 [16384, 1], P(('gx', 'gy')), may hold values from 0 to 127; in each aligned block of 128 rows (0 to 127, 128 to 255, ...) at most 2 rows name the same one
- cells: int32 [2097152], P(('gx', 'gy')), may hold values from 0 to 65535
Outputs:
- spectrum: float32 [2, 6, 64, 1024, 128], P(None, None, 'gx', 'gy')
The draws below stay inside these ranges and needn't reach their ends.
Inputs may be any that keep to these rules, and one draw needn't show every extreme that they name: owners numbers devices as gx index times the size of gy plus gy index; among the 128 blocks of one device at most 2 have the same owner, and some device has exactly 2 blocks for one owner. cells numbers the cells of the owner's block as (x * 64 + y) * 128 + z.
All inputs are finite; a program needn't handle non-finite values.
Results may differ from the reference program's by a relative error of at most 0.0029.
Values may be sent and summed in bfloat16 or wider, within the bound.
A program may use at most 128 MiB of HBM per device.

```python
import math
import jax
import jax.numpy as jnp
import numpy as np

CX = 8
CY = 64
NZ = 128
BP = 128
CAP = 2
NB = 128
NX = 64
NY = 1024
POINTS = 2097152
N_GX = 8
N_GY = 16


def place_ends(drawn, key, low, top_value):
    spot = [jax.random.randint(jax.random.fold_in(key, axis), (), 0, length) for axis, length in enumerate(drawn.shape)]
    main_axis = drawn.shape.index(max(drawn.shape))
    next_to = spot[:main_axis] + [(spot[main_axis] + 1) % drawn.shape[main_axis]] + spot[main_axis + 1:]
    return drawn.at[tuple(spot)].set(low).at[tuple(next_to)].set(top_value)


def block_levels(own_key, extent, split, low, top_value):
    loudness = 1.0
    for axis_at, parts in split:
        heights = jax.random.uniform(jax.random.fold_in(jax.random.fold_in(own_key, 6), axis_at), (parts,), jnp.float32, low / len(split), top_value / len(split))
        loudness = loudness * jnp.repeat(jnp.exp(heights), extent[axis_at] // parts).reshape((-1,) + (1,) * (len(extent) - 1 - axis_at))
    return loudness


def shared_out(rng, own, number, rows, number_of, top, most, skew):
    sequence = jax.random.permutation(rng, number_of)
    heavy_load, ordinary = portions_of(number_of, rows * top, most, skew, True), portions_of(number_of, rows * top, most, skew, False)
    places = jnp.arange(number_of)

    def named(lengths, turn):
        used = int((lengths > 0).sum())
        fixed = max(1, used // 4)
        shifted = fixed + (places - fixed + turn * (used - fixed)) % max(1, number_of - fixed)
        return jnp.zeros((number_of,), jnp.int32).at[sequence[jnp.where(places < fixed, places, shifted)]].set(jnp.asarray(lengths, jnp.int32))

    lengths = jnp.where(number % 4 == 0, named(heavy_load, number // 4), named(ordinary, number - number // 4 - 1))
    mixed = jax.random.permutation(jax.random.fold_in(own, 3), number_of)
    donor, taker = mixed[0:number_of // 2 * 2:2], mixed[1:number_of // 2 * 2:2]
    slack = jnp.minimum(lengths[donor] - 1, most - lengths[taker]) // 2
    slack = jnp.where((donor == sequence[0]) | (taker == sequence[0]) | (lengths[taker] == 0), 0, jnp.maximum(slack, 0))
    shifted = jax.random.randint(jax.random.fold_in(own, 4), (number_of // 2,), 0, 1 << 20) % (slack + 1)
    lengths = lengths.at[donor].add(-shifted).at[taker].add(shifted)
    items = jnp.searchsorted(jnp.cumsum(lengths), jnp.arange(rows * top), side="right").astype(jnp.int32)
    table = items.reshape(top, rows).T
    table = table[jax.random.permutation(jax.random.fold_in(own, 1), rows)]
    turn = jax.random.randint(jax.random.fold_in(own, 2), (rows, 1), 0, top)
    return jnp.take_along_axis(table, (jnp.arange(top)[None, :] + turn) % top, axis=1)


def portions_of(count, total, bound, lean, full):
    loads = [(1 << 20) // math.isqrt(standing ** lean) + 1 for standing in range(1, count + 1)]
    largest = bound if full else min(bound, max(-(-total // count), total * loads[0] // sum(loads)))
    least = 1 if total - largest >= count - 1 else 0
    holding, spare = [largest] + [least] * (count - 1), total - largest - least * (count - 1)
    while spare > 0:
        candidates = [i for i in range(1, count) if holding[i] < largest] or [i for i in range(1, count) if holding[i] < bound]
        pool, left = sum([loads[i] for i in candidates]), spare
        for i in candidates:
            addition = min(bound - holding[i], max(1, left * loads[i] // pool), spare)
            holding[i] = holding[i] + addition
            spare = spare - addition
    return np.array(holding)


def scatter_about(rng, shape, spread, limit, split=(), held_as=jnp.bfloat16):
    level = block_levels(rng, shape, split, -0.22, 0.18) if split else 1.0
    values = jax.random.normal(rng, shape, jnp.float32) * spread * level
    return jnp.minimum(jnp.maximum(values, -limit), limit).astype(held_as)


def setup_inputs(seed: int = 0) -> dict:
    keys = jax.random.split(jax.random.key(seed), 5)
    offsets = scatter_about(keys[0], (3, POINTS), 1.0, 5.0, ((1, 128),), jnp.float32)
    weights = jnp.clip(jax.random.uniform(keys[1], (POINTS,), jnp.float32, -1.0, 1.0) * block_levels(keys[1], (POINTS,), ((0, 128),), -0.4, 0.0), -1.0, 1.0)
    owners_keys = jax.random.split(jax.random.fold_in(keys[2], 1), (N_GX * N_GY * NB) // NB)
    owners_turns = jax.random.permutation(jax.random.fold_in(keys[2], 3), (N_GX * N_GY * NB) // NB)
    owners = jax.vmap(lambda own, number: shared_out(jax.random.fold_in(keys[2], 2), own, number, NB, N_GX * N_GY, 1, CAP, 1))(owners_keys, owners_turns).reshape((N_GX * N_GY * NB, 1))
    cells = place_ends(jax.random.randint(keys[3], (POINTS,), 0, CX * CY * NZ), jax.random.fold_in(keys[3], 1), 0, (CX * CY * NZ) - 1).astype(jnp.int32)
    return dict(offsets=offsets, weights=weights, owners=owners, cells=cells)


def quad_terms(offsets, weights):
    along_x = offsets[0]
    along_y = offsets[1]
    along_z = offsets[2]
    scaled = weights / jnp.maximum(along_x * along_x + along_y * along_y + along_z * along_z, 0.25)
    return jnp.stack([along_x * along_x * scaled, along_y * along_y * scaled, along_z * along_z * scaled,
                      along_x * along_y * scaled, along_y * along_z * scaled, along_z * along_x * scaled]).astype(jnp.bfloat16)


def flip_bits(value, width):
    result = 0
    for position_bit in range(width):
        result = result + ((value >> position_bit) & 1) * (1 << (width - 1 - position_bit))
    return result


def frequency_table(groups, per_group):
    width = groups.bit_length() - 1
    return np.array([flip_bits(entry_index // per_group, width) + groups * (entry_index % per_group)
                     for entry_index in range(groups * per_group)], dtype=np.int64)


def reference(offsets, weights, owners, cells):
    quadratic = quad_terms(offsets, weights).astype(jnp.float32)
    target = jnp.repeat(owners[:, 0], BP)
    owner_x = target // N_GY
    owner_y = target % N_GY
    row_local = cells // NZ
    depth_index = cells % NZ
    grid_x = owner_x * CX + row_local // CY
    grid_y = owner_y * CY + row_local % CY
    flat_index = ((grid_x * NY + grid_y) * NZ + depth_index).astype(jnp.int32)
    summed = jax.ops.segment_sum(quadratic.T, flat_index, num_segments=NX * NY * NZ)
    fields = jnp.transpose(summed.reshape(NX, NY, NZ, 6), (3, 0, 1, 2))
    transformed = jnp.fft.fft(fields, axis=2)
    freq_order = frequency_table(N_GY, CY)
    transformed = transformed[:, :, freq_order, :]
    return jnp.stack([jnp.real(transformed), jnp.imag(transformed)]).astype(jnp.float32)
```

```python
import functools
import math

import jax
import jax.numpy as jnp
import numpy as np
from jax import lax
from jax.experimental import pallas as pl
from jax.experimental.pallas import tpu as pltpu
from jax.sharding import PartitionSpec as P

CX = 8
CY = 64
NZ = 128
BP = 128
CAP = 2
NB = 128
N_GX = 8
N_GY = 16
DEVICES = N_GX * N_GY
ROWS = CX * CY
SHARE = ROWS // N_GY
PASSES = 3
LANES = 2 * NZ
MESH = pl.DeviceIdType.MESH
VMEM = pl.BlockSpec(memory_space=pltpu.VMEM)
ANY = pl.BlockSpec(memory_space=pl.ANY)


def reversed4(value):
    return value % 2 * 8 + value // 2 % 2 * 4 + value // 4 % 2 * 2 + value // 8


def pack_kernel(owner_ref, off_ref, weight_ref, cell_ref, send_ref, count_ref):
    def clear_count(i, carry):
        count_ref[i] = 0
        return carry

    lax.fori_loop(0, DEVICES, clear_count, 0, unroll=8)
    send_ref[...] = jnp.zeros_like(send_ref)
    plane = lax.broadcasted_iota(jnp.int32, (8, BP), 0)
    third = plane % 3

    def block(b, carry):
        owner = owner_ref[b]
        rank = count_ref[owner]
        count_ref[owner] = rank + 1
        lanes = pl.ds(pl.multiple_of(b * BP, BP), BP)
        a = jnp.broadcast_to(off_ref[0:1, lanes], (8, BP))
        bb = jnp.broadcast_to(off_ref[1:2, lanes], (8, BP))
        c = jnp.broadcast_to(off_ref[2:3, lanes], (8, BP))
        w = jnp.broadcast_to(weight_ref[pl.ds(b, 1), :], (8, BP))
        cell = jnp.broadcast_to(cell_ref[pl.ds(b, 1), :], (8, BP))
        scaled = w / jnp.maximum(a * a + bb * bb + c * c, 0.25)
        first = jnp.where(third == 0, a, jnp.where(third == 1, bb, c))
        after = jnp.where(third == 0, bb, jnp.where(third == 1, c, a))
        value = first * jnp.where(plane < 3, first, after) * scaled
        code = jnp.where(plane == 6, cell // NZ - ROWS // 2, cell % NZ).astype(jnp.float32)
        value = jnp.where(plane < 6, value, code)
        send_ref[owner, rank] = value.astype(jnp.bfloat16)
        return carry

    lax.fori_loop(0, NB, block, 0, unroll=4)


def real_transform(values):
    count = len(values)
    if count == 2:
        return [(values[0] + values[1], None), (values[0] - values[1], None)]
    even = real_transform(values[::2])
    odd = real_transform(values[1::2])
    half = count // 2

    def at(spectrum, k):
        if k <= half // 2:
            return spectrum[k]
        re, im = spectrum[half - k]
        return re, None if im is None else -im

    result = []
    for k in range(half + 1):
        ere, eim = at(even, k % half)
        ore, oim = at(odd, k % half)
        if k == 0 or k == half:
            pre, pim = (ore, oim) if k == 0 else (-ore, None if oim is None else -oim)
        elif 4 * k == count:
            pre, pim = (oim, -ore)
        else:
            angle = 2.0 * math.pi * k / count
            cos, sin = math.cos(angle), math.sin(angle)
            if oim is None:
                pre, pim = ore * cos, ore * -sin
            else:
                pre, pim = ore * cos + oim * sin, oim * cos - ore * sin

        def plus(u, v):
            return v if u is None else u if v is None else u + v

        result.append((plus(ere, pre), plus(eim, pim)))
    return result


def exchange_kernel(
    send_ref, out_ref, recv, acc, field, gathered, partial, route_send, route_recv, sends, recvs
):
    gx = lax.axis_index("gx")
    gy = lax.axis_index("gy")
    me = gx * N_GY + gy
    own = pltpu.make_async_copy(send_ref.at[me], recv.at[me], route_recv.at[0])
    own.start()

    def route(j, first):
        to_x = (gx + j) % N_GX

        def one(i, carry):
            to_y = (gy + i) % N_GY
            pltpu.make_async_remote_copy(
                src_ref=send_ref.at[to_x * N_GY + to_y],
                dst_ref=recv.at[me],
                send_sem=route_send,
                recv_sem=route_recv.at[j],
                device_id=(to_x, to_y),
                device_id_type=MESH,
            ).start()
            return carry

        lax.fori_loop(first, N_GY, one, 0)

    route(0, 1)

    def route_all(j, carry):
        route(j, 0)
        return carry

    lax.fori_loop(1, N_GX, route_all, 0)

    row_index = lax.broadcasted_iota(jnp.int32, (ROWS, BP), 0) - ROWS // 2
    row_index = row_index.astype(jnp.float32).astype(jnp.bfloat16)
    depth_index = lax.broadcasted_iota(jnp.int32, (NZ, BP), 0)
    depth_index = depth_index.astype(jnp.float32).astype(jnp.bfloat16)
    one_value = jnp.ones((), jnp.bfloat16)
    zero_value = jnp.zeros((), jnp.bfloat16)

    def deposit(part, j):
        base = (gx + N_GX - j) % N_GX * N_GY
        row_hot, spread = [], []
        for slot in range(N_GY * CAP):
            block = recv[base + slot // CAP, slot % CAP]
            row = jnp.broadcast_to(block[6:7], (ROWS, BP))
            depth = jnp.broadcast_to(block[7:8], (NZ, BP)) == depth_index
            row_hot.append(jnp.where(row == row_index, one_value, zero_value))
            pair = [
                jnp.where(depth, jnp.broadcast_to(block[k : k + 1], (NZ, BP)), zero_value)
                for k in (2 * part, 2 * part + 1)
            ]
            spread.append(jnp.concatenate(pair, axis=0))
        acc[...] += lax.dot_general(
            jnp.concatenate(row_hot, axis=1),
            jnp.concatenate(spread, axis=1),
            (((1,), (1,)), ((), ())),
            preferred_element_type=jnp.float32,
        )

    def scatter_fields(part):
        for i in range(N_GY):
            field[part, i] = acc[i * SHARE : (i + 1) * SHARE].astype(jnp.bfloat16)
        pltpu.make_async_copy(
            field.at[part, gy], gathered.at[part, gy], recvs.at[0, part]
        ).start()

        def one(i, carry):
            to_y = (gy + i) % N_GY
            pltpu.make_async_remote_copy(
                src_ref=field.at[part, to_y],
                dst_ref=gathered.at[part, gy],
                send_sem=sends.at[0, part],
                recv_sem=recvs.at[0, part],
                device_id=(gx, to_y),
                device_id_type=MESH,
            ).start()
            return carry

        lax.fori_loop(1, N_GY, one, 0)

    def frequency_slot(device):
        freq = reversed4(device)
        return 8 - (freq - 8) * (2 * (freq // 8) - 1)

    def transform(part):
        pltpu.make_async_copy(gathered.at[part], gathered.at[part], recvs.at[0, part]).wait()
        for rows in range(SHARE // 16):
            for lanes in range(LANES // 128):
                at = (slice(16 * rows, 16 * rows + 16), slice(128 * lanes, 128 * lanes + 128))
                values = [gathered[(part, s) + at].astype(jnp.float32) for s in range(N_GY)]
                for r, (re, im) in enumerate(real_transform(values)):
                    im = jnp.zeros_like(re) if im is None else im
                    partial[(part, r, 0) + at] = re.astype(jnp.bfloat16)
                    partial[(part, r, 1) + at] = im.astype(jnp.bfloat16)
        pltpu.make_async_copy(
            partial.at[part, frequency_slot(gy)], out_ref.at[part, gy], recvs.at[1, part]
        ).start()

        def one(i, carry):
            to_y = (gy + i) % N_GY
            pltpu.make_async_remote_copy(
                src_ref=partial.at[part, frequency_slot(to_y)],
                dst_ref=out_ref.at[part, gy],
                send_sem=sends.at[1, part],
                recv_sem=recvs.at[1, part],
                device_id=(gx, to_y),
                device_id_type=MESH,
            ).start()
            return carry

        lax.fori_loop(1, N_GY, one, 0)

    for part in range(PASSES):
        acc[...] = jnp.zeros_like(acc)

        def step(j, carry):
            if part == 0:
                arrived = recv.at[pl.ds(0, N_GY)]
                pltpu.make_async_copy(arrived, arrived, route_recv.at[j]).wait()
            deposit(part, j)
            return carry

        if part == 0:
            lax.fori_loop(0, N_GX, step, 0)
        else:
            lax.fori_loop(0, N_GX // 2, step, 0)
            transform(part - 1)
            lax.fori_loop(N_GX // 2, N_GX, step, 0)
        scatter_fields(part)
    transform(PASSES - 1)

    sent = send_ref.at[pl.ds(0, DEVICES - 1)]
    pltpu.make_async_copy(sent, sent, route_send).wait()
    for part in range(PASSES):
        sent = field.at[part, pl.ds(0, N_GY - 1)]
        pltpu.make_async_copy(sent, sent, sends.at[0, part]).wait()
        sent = out_ref.at[part, pl.ds(0, N_GY - 1)]
        pltpu.make_async_copy(sent, sent, sends.at[1, part]).wait()
        pltpu.make_async_copy(out_ref.at[part], out_ref.at[part], recvs.at[1, part]).wait()


def lines_kernel(table_ref, part_ref, out_ref, matrix, sem):
    freq = reversed4(lax.axis_index("gy"))

    @pl.when(pl.program_id(0) == 0)
    def _():
        copy = pltpu.make_async_copy(table_ref.at[freq], matrix, sem)
        copy.start()
        copy.wait()

    for x in range(CX):
        values = part_ref[0, 2 * x : 2 * x + 2].reshape(2 * CY, LANES)
        lines = jnp.dot(matrix[0], values, preferred_element_type=jnp.float32)
        lines += jnp.dot(matrix[1], values, preferred_element_type=jnp.float32)
        for half in range(2):
            for k in range(2):
                out_ref[half, k, x] = lines[half * CY : half * CY + CY, k * NZ : k * NZ + NZ]


def line_table():
    y = np.arange(CY)
    q = np.arange(CY)
    tables = []
    for freq in range(N_GY):
        phase = (q[:, None] * N_GY + freq) * y[None, :] % (CY * N_GY)
        angle = phase * (2.0 * np.pi / (CY * N_GY))
        cos, sin = np.cos(angle), np.sin(angle)
        sign = -1.0 if freq > N_GY // 2 else 1.0
        full = np.stack([np.stack([cos, sign * sin], 1), np.stack([-sin, sign * cos], 1)])
        full = full.reshape(2, CY, 2, 2, CY // 2).transpose(0, 1, 3, 2, 4).reshape(2 * CY, 2 * CY)
        high = full.astype(jnp.bfloat16)
        tables.append(np.stack([high, (full - high.astype(np.float64)).astype(jnp.bfloat16)]))
    return np.stack(tables)


def shards(table, offsets, weights, owners, cells):
    send = pl.pallas_call(
        pack_kernel,
        out_shape=jax.ShapeDtypeStruct((DEVICES, CAP, 8, BP), jnp.bfloat16),
        in_specs=[pl.BlockSpec(memory_space=pltpu.SMEM), VMEM, VMEM, VMEM],
        out_specs=VMEM,
        scratch_shapes=[pltpu.SMEM((DEVICES,), jnp.int32)],
        name="pack",
    )(owners.reshape(NB), offsets, weights.reshape(NB, BP), cells.reshape(NB, BP))
    partial = pl.pallas_call(
        exchange_kernel,
        out_shape=jax.ShapeDtypeStruct((PASSES, N_GY, 2, SHARE, LANES), jnp.bfloat16),
        in_specs=[VMEM],
        out_specs=ANY,
        scratch_shapes=[
            pltpu.VMEM((DEVICES, CAP, 8, BP), jnp.bfloat16),
            pltpu.VMEM((ROWS, LANES), jnp.float32),
            pltpu.VMEM((PASSES, N_GY, SHARE, LANES), jnp.bfloat16),
            pltpu.VMEM((PASSES, N_GY, SHARE, LANES), jnp.bfloat16),
            pltpu.VMEM((PASSES, N_GY // 2 + 1, 2, SHARE, LANES), jnp.bfloat16),
            pltpu.SemaphoreType.DMA,
            pltpu.SemaphoreType.DMA((N_GX,)),
            pltpu.SemaphoreType.DMA((2, PASSES)),
            pltpu.SemaphoreType.DMA((2, PASSES)),
        ],
        compiler_params=pltpu.CompilerParams(has_side_effects=True, vmem_limit_bytes=60 << 20),
        name="exchange",
    )(send)
    return pl.pallas_call(
        lines_kernel,
        grid=(PASSES,),
        out_shape=jax.ShapeDtypeStruct((2, 6, CX, CY, NZ), jnp.float32),
        in_specs=[ANY, pl.BlockSpec((1, N_GY, 2, SHARE, LANES), lambda c: (c, 0, 0, 0, 0))],
        out_specs=pl.BlockSpec((2, 2, CX, CY, NZ), lambda c: (0, c, 0, 0, 0)),
        scratch_shapes=[
            pltpu.VMEM((2, 2 * CY, 2 * CY), jnp.bfloat16),
            pltpu.SemaphoreType.DMA,
        ],
        name="lines",
    )(table, partial)


def solution(mesh):
    table = line_table()
    placed = (P(None, ("gx", "gy")), P(("gx", "gy")), P(("gx", "gy"), None), P(("gx", "gy")))
    mapped = jax.shard_map(
        shards,
        mesh=mesh,
        in_specs=(P(),) + placed,
        out_specs=P(None, None, "gx", "gy", None),
        check_vma=False,
    )
    return functools.partial(mapped, jnp.asarray(table))
```

```python
import functools
import math

import jax
import jax.numpy as jnp
import numpy as np
from jax import lax
from jax.experimental import pallas as pl
from jax.experimental.pallas import tpu as pltpu
from jax.sharding import PartitionSpec as P

CX = 8
CY = 64
NZ = 128
BP = 128
CAP = 2
NB = 128
N_GX = 8
N_GY = 16
DEVICES = N_GX * N_GY
ROWS = CX * CY
LANES = 2 * NZ
GRANULE = 16
UNITS = ((0, 0, ROWS), (1, 0, ROWS), (2, 0, ROWS // 2), (2, ROWS // 2, ROWS // 2))
MESH = pl.DeviceIdType.MESH
ANY = pl.BlockSpec(memory_space=pl.ANY)


def granules(unit):
    return unit[2] // (N_GY * GRANULE)


def reversed4(value):
    return value % 2 * 8 + value // 2 % 2 * 4 + value // 4 % 2 * 2 + value // 8


def real_transform(values):
    count = len(values)
    if count == 2:
        return [(values[0] + values[1], None), (values[0] - values[1], None)]
    even = real_transform(values[::2])
    odd = real_transform(values[1::2])
    half = count // 2

    def at(spectrum, k):
        if k <= half // 2:
            return spectrum[k]
        re, im = spectrum[half - k]
        return re, None if im is None else -im

    result = []
    for k in range(half + 1):
        ere, eim = at(even, k % half)
        ore, oim = at(odd, k % half)
        if k == 0 or k == half:
            pre, pim = (ore, oim) if k == 0 else (-ore, None if oim is None else -oim)
        elif 4 * k == count:
            pre, pim = (oim, -ore)
        else:
            angle = 2.0 * math.pi * k / count
            cos, sin = math.cos(angle), math.sin(angle)
            if oim is None:
                pre, pim = ore * cos, ore * -sin
            else:
                pre, pim = ore * cos + oim * sin, oim * cos - ore * sin

        def plus(u, v):
            return v if u is None else u if v is None else u + v

        result.append((plus(ere, pre), plus(eim, pim)))
    return result


def write_slots(owner, offsets, weights, cells, planes, send_ref):
    a, b, c = (offsets[:, i, :] for i in range(3))
    scaled = weights / jnp.maximum(a * a + b * b + c * c, 0.25)
    pairs = ((a, a), (b, b), (c, c), (a, b), (b, c), (c, a))
    values = [(first * second * scaled).astype(jnp.bfloat16) for first, second in pairs]
    row = (cells >> 7) - ROWS // 2
    values += [code.astype(jnp.float32).astype(jnp.bfloat16) for code in (row, cells & (NZ - 1))]
    across = jnp.broadcast_to(owner.astype(jnp.float32), (NB, NB))
    same = jnp.where(across == across.T, 1.0, 0.0)
    block = lax.broadcasted_iota(jnp.int32, (NB, NB), 0)
    before = jnp.where(block < lax.broadcasted_iota(jnp.int32, (NB, NB), 1), same, 0.0)
    slot = owner.astype(jnp.float32) * CAP + jnp.sum(before, axis=0, keepdims=True)
    slots = lax.broadcasted_iota(jnp.int32, (DEVICES * CAP, NB), 0).astype(jnp.float32)
    hot = jnp.where(slots == slot, 1.0, 0.0).astype(jnp.bfloat16)
    for k, value in enumerate(values):
        placed = jnp.dot(hot, value, preferred_element_type=jnp.float32)
        planes[pl.ds(k, DEVICES * CAP, stride=8), :] = placed
    send_ref[...] = planes[...].reshape(DEVICES, CAP, 8, BP).astype(jnp.bfloat16)


def exchange_kernel(owner_hbm, offset_hbm, weight_hbm, cell_hbm, *refs):
    count = len(UNITS)
    outs, refs = refs[:count], refs[count:]
    fields, refs = refs[:count], refs[count:]
    gathered, refs = refs[:count], refs[count:]
    partials, refs = refs[:count], refs[count:]
    owner_ref, offset_ref, weight_ref, cell_ref, planes, send_ref, recv, acc = refs[:8]
    load_sems, route_send, route_recv, sends, recvs = refs[8:]
    gx = lax.axis_index("gx")
    gy = lax.axis_index("gy")
    me = gx * N_GY + gy

    loads = [
        pltpu.make_async_copy(source, target, load_sems.at[i])
        for i, (source, target) in enumerate(
            (
                (owner_hbm, owner_ref),
                (offset_hbm, offset_ref),
                (weight_hbm, weight_ref),
                (cell_hbm, cell_ref),
            )
        )
    ]
    for load in loads:
        load.start()
    barrier = pltpu.get_barrier_semaphore()

    def greet(i, carry):
        other = (me + i) % DEVICES
        pl.semaphore_signal(
            barrier, inc=1, device_id=(other // N_GY, other % N_GY), device_id_type=MESH
        )
        return carry

    lax.fori_loop(1, DEVICES, greet, 0)
    for load in loads:
        load.wait()
    write_slots(owner_ref[...], offset_ref, weight_ref[...], cell_ref[...], planes, send_ref)
    pl.semaphore_wait(barrier, DEVICES - 1)

    pltpu.make_async_copy(send_ref.at[me], recv.at[me], route_recv.at[0]).start()

    def route(j, first):
        to_x = (gx + j) % N_GX

        def one(i, carry):
            to_y = (gy + i) % N_GY
            pltpu.make_async_remote_copy(
                src_ref=send_ref.at[to_x * N_GY + to_y],
                dst_ref=recv.at[me],
                send_sem=route_send,
                recv_sem=route_recv.at[j],
                device_id=(to_x, to_y),
                device_id_type=MESH,
            ).start()
            return carry

        lax.fori_loop(first, N_GY, one, 0)

    route(0, 1)

    def route_all(j, carry):
        route(j, 0)
        return carry

    lax.fori_loop(1, N_GX, route_all, 0)

    depth_index = lax.broadcasted_iota(jnp.int32, (NZ, BP), 0)
    depth_index = depth_index.astype(jnp.float32).astype(jnp.bfloat16)
    one_value = jnp.ones((), jnp.bfloat16)
    zero_value = jnp.zeros((), jnp.bfloat16)

    def deposit(unit, first, phases):
        pair, low, rows = unit
        row_index = lax.broadcasted_iota(jnp.int32, (rows, BP), 0) + (low - ROWS // 2)
        row_index = row_index.astype(jnp.float32).astype(jnp.bfloat16)
        row_hot, spread = [], []
        for phase in range(phases):
            base = (gx + N_GX - (first + phase)) % N_GX * N_GY
            for slot in range(N_GY * CAP):
                block = recv[base + slot // CAP, slot % CAP]
                row = jnp.broadcast_to(block[6:7], (rows, BP))
                depth = jnp.broadcast_to(block[7:8], (NZ, BP)) == depth_index
                row_hot.append(jnp.where(row == row_index, one_value, zero_value))
                terms = [
                    jnp.where(depth, jnp.broadcast_to(block[k : k + 1], (NZ, BP)), zero_value)
                    for k in (2 * pair, 2 * pair + 1)
                ]
                spread.append(jnp.concatenate(terms, axis=0))
        acc[:rows] += lax.dot_general(
            jnp.concatenate(row_hot, axis=1),
            jnp.concatenate(spread, axis=1),
            (((1,), (1,)), ((), ())),
            preferred_element_type=jnp.float32,
        )

    def to_peers(sources, target, slot_of, stage, unit_index):
        pltpu.make_async_copy(
            sources.at[slot_of(gy)], target.at[gy], recvs.at[stage, unit_index]
        ).start()

        def one(i, carry):
            to_y = (gy + i) % N_GY
            pltpu.make_async_remote_copy(
                src_ref=sources.at[slot_of(to_y)],
                dst_ref=target.at[gy],
                send_sem=sends.at[stage, unit_index],
                recv_sem=recvs.at[stage, unit_index],
                device_id=(gx, to_y),
                device_id_type=MESH,
            ).start()
            return carry

        lax.fori_loop(1, N_GY, one, 0)

    def scatter_fields(u):
        parts = granules(UNITS[u])
        for i in range(N_GY):
            for g in range(parts):
                start = (i * parts + g) * GRANULE
                fields[u][i, g] = acc[start : start + GRANULE].astype(jnp.bfloat16)
        to_peers(fields[u], gathered[u], lambda device: device, 0, u)

    def frequency_slot(device):
        freq = reversed4(device)
        return 8 - (freq - 8) * (2 * (freq // 8) - 1)

    def transform(u):
        pltpu.make_async_copy(gathered[u], gathered[u], recvs.at[0, u]).wait()
        for g in range(granules(UNITS[u])):
            for half in range(LANES // 128):
                lanes = slice(128 * half, 128 * half + 128)
                values = [gathered[u][s, g, :, lanes].astype(jnp.float32) for s in range(N_GY)]
                for r, (re, im) in enumerate(real_transform(values)):
                    im = jnp.zeros_like(re) if im is None else im
                    partials[u][r, g, 0, :, lanes] = re.astype(jnp.bfloat16)
                    partials[u][r, g, 1, :, lanes] = im.astype(jnp.bfloat16)
        to_peers(partials[u], outs[u], frequency_slot, 1, u)

    def run(u, first, last, phases):
        def step(i, carry):
            if u == 0:
                arrived = recv.at[pl.ds(0, N_GY)]
                pltpu.make_async_copy(arrived, arrived, route_recv.at[i]).wait()
            deposit(UNITS[u], i * phases, phases)
            return carry

        lax.fori_loop(first // phases, last // phases, step, 0)

    for u in range(count):
        acc[...] = jnp.zeros_like(acc)
        if u == 0:
            run(u, 0, N_GX, 1)
        elif u == 2:
            run(u, 0, N_GX, 2)
        else:
            run(u, 0, N_GX // 2, 2)
            transform(u - 1)
            run(u, N_GX // 2, N_GX, 2)
        scatter_fields(u)
        if u == 2:
            transform(u - 1)
    transform(count - 1)

    sent = send_ref.at[pl.ds(0, DEVICES - 1)]
    pltpu.make_async_copy(sent, sent, route_send).wait()
    for u in range(count):
        sent = fields[u].at[pl.ds(0, N_GY - 1)]
        pltpu.make_async_copy(sent, sent, sends.at[0, u]).wait()
        sent = outs[u].at[pl.ds(0, N_GY - 1)]
        pltpu.make_async_copy(sent, sent, sends.at[1, u]).wait()
        pltpu.make_async_copy(outs[u], outs[u], recvs.at[1, u]).wait()


def lines_kernel(table_ref, *refs):
    count = len(UNITS)
    parts, refs = refs[:count], refs[count:]
    out_ref, refs = refs[0], refs[1:]
    held, refs = refs[:count], refs[count:]
    matrix, staged, load_sems, store_sem = refs
    freq = reversed4(lax.axis_index("gy"))
    loads = [pltpu.make_async_copy(table_ref.at[freq], matrix, load_sems.at[count])]
    loads += [pltpu.make_async_copy(parts[u], held[u], load_sems.at[u]) for u in range(count)]
    for load in loads:
        load.start()
    loads[0].wait()
    for u, (pair, low, rows) in enumerate(UNITS):
        loads[1 + u].wait()
        sources = N_GY * CY // rows
        for x in range(rows // CY):
            values = held[u][sources * x : sources * x + sources].reshape(2 * CY, LANES)
            lines = jnp.dot(matrix[0], values, preferred_element_type=jnp.float32)
            lines += jnp.dot(matrix[1], values, preferred_element_type=jnp.float32)
            to_x = low // CY + x
            for half in range(2):
                for k in range(2):
                    staged[half, 2 * pair + k, to_x] = lines[
                        half * CY : half * CY + CY, k * NZ : k * NZ + NZ
                    ]
            if x % 4 == 3:
                for half in range(2):
                    at = (half, pl.ds(2 * pair, 2), pl.ds(to_x - 3, 4))
                    pltpu.make_async_copy(staged.at[at], out_ref.at[at], store_sem).start()
    pltpu.make_async_copy(staged, out_ref, store_sem).wait()


def line_table():
    y = np.arange(CY)
    q = np.arange(CY)
    tables = []
    for freq in range(N_GY):
        phase = (q[:, None] * N_GY + freq) * y[None, :] % (CY * N_GY)
        angle = phase * (2.0 * np.pi / (CY * N_GY))
        cos, sin = np.cos(angle), np.sin(angle)
        sign = -1.0 if freq > N_GY // 2 else 1.0
        full = np.stack([np.stack([cos, sign * sin], 1), np.stack([-sin, sign * cos], 1)])
        full = full.reshape(2, CY, 2, CY // GRANULE, GRANULE).transpose(0, 1, 3, 2, 4)
        full = full.reshape(2 * CY, 2 * CY)
        high = full.astype(jnp.bfloat16)
        tables.append(np.stack([high, (full - high.astype(np.float64)).astype(jnp.bfloat16)]))
    return np.stack(tables)


def shards(table, offsets, weights, owners, cells):
    unit_shapes = [(N_GY, granules(unit), GRANULE, LANES) for unit in UNITS]
    half_shapes = [(9, granules(unit), 2, GRANULE, LANES) for unit in UNITS]
    out_shapes = [(N_GY, granules(unit), 2, GRANULE, LANES) for unit in UNITS]
    parts = pl.pallas_call(
        exchange_kernel,
        out_shape=[jax.ShapeDtypeStruct(shape, jnp.bfloat16) for shape in out_shapes],
        in_specs=[ANY] * 4,
        out_specs=[ANY] * len(UNITS),
        scratch_shapes=[
            *[pltpu.VMEM(shape, jnp.bfloat16) for shape in unit_shapes],
            *[pltpu.VMEM(shape, jnp.bfloat16) for shape in unit_shapes],
            *[pltpu.VMEM(shape, jnp.bfloat16) for shape in half_shapes],
            pltpu.VMEM((1, NB), jnp.int32),
            pltpu.VMEM((NB, 3, BP), jnp.float32),
            pltpu.VMEM((NB, BP), jnp.float32),
            pltpu.VMEM((NB, BP), jnp.int32),
            pltpu.VMEM((DEVICES * CAP * 8, BP), jnp.float32),
            pltpu.VMEM((DEVICES, CAP, 8, BP), jnp.bfloat16),
            pltpu.VMEM((DEVICES, CAP, 8, BP), jnp.bfloat16),
            pltpu.VMEM((ROWS, LANES), jnp.float32),
            pltpu.SemaphoreType.DMA((4,)),
            pltpu.SemaphoreType.DMA,
            pltpu.SemaphoreType.DMA((N_GX,)),
            pltpu.SemaphoreType.DMA((2, len(UNITS))),
            pltpu.SemaphoreType.DMA((2, len(UNITS))),
        ],
        compiler_params=pltpu.CompilerParams(
            has_side_effects=True, collective_id=0, vmem_limit_bytes=60 << 20
        ),
        name="exchange",
    )(
        owners.reshape(1, NB),
        jnp.transpose(offsets.reshape(3, NB, BP), (1, 0, 2)),
        weights.reshape(NB, BP),
        cells.reshape(NB, BP),
    )
    return pl.pallas_call(
        lines_kernel,
        out_shape=jax.ShapeDtypeStruct((2, 6, CX, CY, NZ), jnp.float32),
        in_specs=[ANY] * (1 + len(UNITS)),
        out_specs=ANY,
        scratch_shapes=[
            *[pltpu.VMEM(shape, jnp.bfloat16) for shape in out_shapes],
            pltpu.VMEM((2, 2 * CY, 2 * CY), jnp.bfloat16),
            pltpu.VMEM((2, 6, CX, CY, NZ), jnp.float32),
            pltpu.SemaphoreType.DMA((1 + len(UNITS),)),
            pltpu.SemaphoreType.DMA,
        ],
        name="lines",
    )(table, *parts)


def solution(mesh):
    table = line_table()
    placed = (P(None, ("gx", "gy")), P(("gx", "gy")), P(("gx", "gy"), None), P(("gx", "gy")))
    mapped = jax.shard_map(
        shards,
        mesh=mesh,
        in_specs=(P(),) + placed,
        out_specs=P(None, None, "gx", "gy", None),
        check_vma=False,
    )
    return functools.partial(mapped, jnp.asarray(table))
```

```python
import functools
import math

import jax
import jax.numpy as jnp
import numpy as np
from jax import lax
from jax.experimental import pallas as pl
from jax.experimental.pallas import tpu as pltpu
from jax.sharding import PartitionSpec as P

CX = 8
CY = 64
NZ = 128
BP = 128
CAP = 2
NB = 128
N_GX = 8
N_GY = 16
DEVICES = N_GX * N_GY
ROWS = CX * CY
LANES = 2 * NZ
GRANULE = 16
HALF = ROWS // 2
UNITS = ((0, 0, HALF), (0, HALF, HALF), (1, 0, ROWS), (2, 0, HALF), (2, HALF, HALF))
MESH = pl.DeviceIdType.MESH
ANY = pl.BlockSpec(memory_space=pl.ANY)
HBM = pl.BlockSpec(memory_space=pltpu.HBM)
VMEM = pl.BlockSpec(memory_space=pltpu.VMEM)


def granules(unit):
    return unit[2] // (N_GY * GRANULE)


def far_first(k, count):
    return count // 2 + (1 - 2 * (k % 2)) * ((k + 1) // 2)


def reversed4(value):
    return value % 2 * 8 + value // 2 % 2 * 4 + value // 4 % 2 * 2 + value // 8


def real_transform(values):
    count = len(values)
    if count == 2:
        return [(values[0] + values[1], None), (values[0] - values[1], None)]
    even = real_transform(values[::2])
    odd = real_transform(values[1::2])
    half = count // 2

    def at(spectrum, k):
        if k <= half // 2:
            return spectrum[k]
        re, im = spectrum[half - k]
        return re, None if im is None else -im

    result = []
    for k in range(half + 1):
        ere, eim = at(even, k % half)
        ore, oim = at(odd, k % half)
        if k == 0 or k == half:
            pre, pim = (ore, oim) if k == 0 else (-ore, None if oim is None else -oim)
        elif 4 * k == count:
            pre, pim = (oim, -ore)
        else:
            angle = 2.0 * math.pi * k / count
            cos, sin = math.cos(angle), math.sin(angle)
            if oim is None:
                pre, pim = ore * cos, ore * -sin
            else:
                pre, pim = ore * cos + oim * sin, oim * cos - ore * sin

        def plus(u, v):
            return v if u is None else u if v is None else u + v

        result.append((plus(ere, pre), plus(eim, pim)))
    return result


def write_slots(owner, offsets, weights, cells, planes, send_ref):
    a, b, c = (offsets[:, i, :] for i in range(3))
    scaled = weights / jnp.maximum(a * a + b * b + c * c, 0.25)
    pairs = ((a, a), (b, b), (c, c), (a, b), (b, c), (c, a))
    values = [(first * second * scaled).astype(jnp.bfloat16) for first, second in pairs]
    row = (cells >> 7) - ROWS // 2
    values += [code.astype(jnp.float32).astype(jnp.bfloat16) for code in (row, cells & (NZ - 1))]
    across = jnp.broadcast_to(owner.astype(jnp.float32), (NB, NB))
    same = jnp.where(across == across.T, 1.0, 0.0)
    block = lax.broadcasted_iota(jnp.int32, (NB, NB), 0)
    before = jnp.where(block < lax.broadcasted_iota(jnp.int32, (NB, NB), 1), same, 0.0)
    slot = owner.astype(jnp.float32) * CAP + jnp.sum(before, axis=0, keepdims=True)
    slots = lax.broadcasted_iota(jnp.int32, (DEVICES * CAP, NB), 0).astype(jnp.float32)
    hot = jnp.where(slots == slot, 1.0, 0.0).astype(jnp.bfloat16)
    for k, value in enumerate(values):
        placed = jnp.dot(hot, value, preferred_element_type=jnp.float32)
        planes[pl.ds(k, DEVICES * CAP, stride=8), :] = placed
    send_ref[...] = planes[...].reshape(DEVICES, CAP, 8, BP).astype(jnp.bfloat16)


def exchange_kernel(owner_hbm, offset_hbm, weight_hbm, cell_hbm, table_hbm, *refs):
    count = len(UNITS)
    outs, refs = refs[:count], refs[count:]
    matrix_ref, refs = refs[0], refs[1:]
    fields, refs = refs[:count], refs[count:]
    gathered, refs = refs[:count], refs[count:]
    partials, refs = refs[:count], refs[count:]
    owner_ref, offset_ref, weight_ref, cell_ref, planes, send_ref, recv, acc = refs[:8]
    load_sems, route_send, route_recv, sends, recvs = refs[8:]
    gx = lax.axis_index("gx")
    gy = lax.axis_index("gy")
    me = gx * N_GY + gy

    loads = [
        pltpu.make_async_copy(source, target, load_sems.at[i])
        for i, (source, target) in enumerate(
            (
                (owner_hbm, owner_ref),
                (offset_hbm, offset_ref),
                (weight_hbm, weight_ref),
                (cell_hbm, cell_ref),
            )
        )
    ]
    for load in loads:
        load.start()
    matrix_load = pltpu.make_async_copy(
        table_hbm.at[reversed4(gy)], matrix_ref, load_sems.at[len(loads)]
    )
    matrix_load.start()
    barrier = pltpu.get_barrier_semaphore()

    def greet(i, carry):
        to_x = (gx + far_first(i // N_GY, N_GX)) % N_GX
        to_y = (gy + far_first(i % N_GY, N_GY)) % N_GY
        pl.semaphore_signal(barrier, inc=1, device_id=(to_x, to_y), device_id_type=MESH)
        return carry

    lax.fori_loop(0, DEVICES - 1, greet, 0)
    for load in loads:
        load.wait()
    write_slots(owner_ref[...], offset_ref, weight_ref[...], cell_ref[...], planes, send_ref)
    pl.semaphore_wait(barrier, DEVICES - 1)

    pltpu.make_async_copy(send_ref.at[me], recv.at[me], route_recv.at[0]).start()

    def route(j, last):
        to_x = (gx + j) % N_GX

        def one(i, carry):
            to_y = (gy + far_first(i, N_GY)) % N_GY
            pltpu.make_async_remote_copy(
                src_ref=send_ref.at[to_x * N_GY + to_y],
                dst_ref=recv.at[me],
                send_sem=route_send,
                recv_sem=route_recv.at[j],
                device_id=(to_x, to_y),
                device_id_type=MESH,
            ).start()
            return carry

        lax.fori_loop(0, last, one, 0)

    route(0, N_GY - 1)

    def route_all(j, carry):
        route(j, N_GY)
        return carry

    lax.fori_loop(1, N_GX, route_all, 0)

    depth_index = lax.broadcasted_iota(jnp.int32, (NZ, BP), 0)
    depth_index = depth_index.astype(jnp.float32).astype(jnp.bfloat16)
    one_value = jnp.ones((), jnp.bfloat16)
    zero_value = jnp.zeros((), jnp.bfloat16)

    def deposit(pair, low, rows, first, phases):
        row_index = lax.broadcasted_iota(jnp.int32, (rows, BP), 0) + (low - ROWS // 2)
        row_index = row_index.astype(jnp.float32).astype(jnp.bfloat16)
        row_hot, spread = [], []
        for phase in range(phases):
            base = (gx + N_GX - (first + phase)) % N_GX * N_GY
            for slot in range(N_GY * CAP):
                block = recv[base + slot // CAP, slot % CAP]
                row = jnp.broadcast_to(block[6:7], (rows, BP))
                depth = jnp.broadcast_to(block[7:8], (NZ, BP)) == depth_index
                row_hot.append(jnp.where(row == row_index, one_value, zero_value))
                terms = [
                    jnp.where(depth, jnp.broadcast_to(block[k : k + 1], (NZ, BP)), zero_value)
                    for k in (2 * pair, 2 * pair + 1)
                ]
                spread.append(jnp.concatenate(terms, axis=0))
        acc[low : low + rows] += lax.dot_general(
            jnp.concatenate(row_hot, axis=1),
            jnp.concatenate(spread, axis=1),
            (((1,), (1,)), ((), ())),
            preferred_element_type=jnp.float32,
        )

    def to_peers(sources, target, slot_of, stage, unit_index):
        pltpu.make_async_copy(
            sources.at[slot_of(gy)], target.at[gy], recvs.at[stage, unit_index]
        ).start()

        def one(i, carry):
            to_y = (gy + far_first(i, N_GY)) % N_GY
            pltpu.make_async_remote_copy(
                src_ref=sources.at[slot_of(to_y)],
                dst_ref=target.at[gy],
                send_sem=sends.at[stage, unit_index],
                recv_sem=recvs.at[stage, unit_index],
                device_id=(gx, to_y),
                device_id_type=MESH,
            ).start()
            return carry

        lax.fori_loop(0, N_GY - 1, one, 0)

    def scatter_fields(u):
        parts = granules(UNITS[u])
        for i in range(N_GY):
            for g in range(parts):
                start = UNITS[u][1] + (i * parts + g) * GRANULE
                fields[u][i, g] = acc[start : start + GRANULE].astype(jnp.bfloat16)
        to_peers(fields[u], gathered[u], lambda device: device, 0, u)

    def frequency_slot(device):
        freq = reversed4(device)
        return 8 - (freq - 8) * (2 * (freq // 8) - 1)

    def transform(u):
        pltpu.make_async_copy(gathered[u], gathered[u], recvs.at[0, u]).wait()
        for g in range(granules(UNITS[u])):
            for half in range(LANES // 128):
                lanes = slice(128 * half, 128 * half + 128)
                values = [gathered[u][s, g, :, lanes].astype(jnp.float32) for s in range(N_GY)]
                for r, (re, im) in enumerate(real_transform(values)):
                    im = jnp.zeros_like(re) if im is None else im
                    partials[u][r, g, 0, :, lanes] = re.astype(jnp.bfloat16)
                    partials[u][r, g, 1, :, lanes] = im.astype(jnp.bfloat16)
        to_peers(partials[u], outs[u], frequency_slot, 1, u)

    def run(pair, low, rows, first, last, phases, arriving=False):
        def step(i, carry):
            if arriving:
                arrived = recv.at[pl.ds(0, N_GY)]
                pltpu.make_async_copy(arrived, arrived, route_recv.at[i]).wait()
            deposit(pair, low, rows, i * phases, phases)
            return carry

        lax.fori_loop(first // phases, last // phases, step, 0)

    acc[...] = jnp.zeros_like(acc)
    run(0, 0, ROWS, 0, 2, 1, arriving=True)
    run(0, 0, HALF, 2, N_GX, 1, arriving=True)
    scatter_fields(0)
    run(0, HALF, HALF, 2, N_GX, 2)
    scatter_fields(1)
    transform(0)
    acc[...] = jnp.zeros_like(acc)
    run(1, 0, ROWS, 0, N_GX // 2, 2)
    transform(1)
    run(1, 0, ROWS, N_GX // 2, N_GX, 2)
    scatter_fields(2)
    acc[...] = jnp.zeros_like(acc)
    run(2, 0, HALF, 0, N_GX, 2)
    scatter_fields(3)
    transform(2)
    run(2, HALF, HALF, 0, N_GX - 2, 2)
    transform(3)
    run(2, HALF, HALF, N_GX - 2, N_GX, 2)
    scatter_fields(4)
    transform(4)
    matrix_load.wait()

    sent = send_ref.at[pl.ds(0, DEVICES - 1)]
    pltpu.make_async_copy(sent, sent, route_send).wait()
    for u in range(count):
        sent = fields[u].at[pl.ds(0, N_GY - 1)]
        pltpu.make_async_copy(sent, sent, sends.at[0, u]).wait()
        sent = outs[u].at[pl.ds(0, N_GY - 1)]
        pltpu.make_async_copy(sent, sent, sends.at[1, u]).wait()
        pltpu.make_async_copy(outs[u], outs[u], recvs.at[1, u]).wait()


def lines_kernel(matrix, *refs):
    parts, (out_ref, staged, store_sem) = refs[: len(UNITS)], refs[len(UNITS) :]
    for u, (pair, low, rows) in enumerate(UNITS):
        sources = N_GY * CY // rows
        for x in range(rows // CY):
            values = parts[u][sources * x : sources * x + sources].reshape(2 * CY, LANES)
            lines = jnp.dot(matrix[0], values, preferred_element_type=jnp.float32)
            lines += jnp.dot(matrix[1], values, preferred_element_type=jnp.float32)
            to_x = low // CY + x
            for half in range(2):
                for k in range(2):
                    staged[half, 2 * pair + k, to_x] = lines[
                        half * CY : half * CY + CY, k * NZ : k * NZ + NZ
                    ]
            if x % 4 == 3:
                for half in range(2):
                    at = (half, pl.ds(2 * pair, 2), pl.ds(to_x - 3, 4))
                    pltpu.make_async_copy(staged.at[at], out_ref.at[at], store_sem).start()
    pltpu.make_async_copy(staged, out_ref, store_sem).wait()


def line_table():
    y = np.arange(CY)
    q = np.arange(CY)
    tables = []
    for freq in range(N_GY):
        phase = (q[:, None] * N_GY + freq) * y[None, :] % (CY * N_GY)
        angle = phase * (2.0 * np.pi / (CY * N_GY))
        cos, sin = np.cos(angle), np.sin(angle)
        sign = -1.0 if freq > N_GY // 2 else 1.0
        full = np.stack([np.stack([cos, sign * sin], 1), np.stack([-sin, sign * cos], 1)])
        full = full.reshape(2, CY, 2, CY // GRANULE, GRANULE).transpose(0, 1, 3, 2, 4)
        full = full.reshape(2 * CY, 2 * CY)
        high = full.astype(jnp.bfloat16)
        tables.append(np.stack([high, (full - high.astype(np.float64)).astype(jnp.bfloat16)]))
    return np.stack(tables)


def shards(table, offsets, weights, owners, cells):
    unit_shapes = [(N_GY, granules(unit), GRANULE, LANES) for unit in UNITS]
    half_shapes = [(9, granules(unit), 2, GRANULE, LANES) for unit in UNITS]
    out_shapes = [(N_GY, granules(unit), 2, GRANULE, LANES) for unit in UNITS]
    *parts, matrix = pl.pallas_call(
        exchange_kernel,
        out_shape=[jax.ShapeDtypeStruct(shape, jnp.bfloat16) for shape in out_shapes]
        + [jax.ShapeDtypeStruct((2, 2 * CY, 2 * CY), jnp.bfloat16)],
        in_specs=[HBM] * 5,
        out_specs=[ANY] * (1 + len(UNITS)),
        scratch_shapes=[
            *[pltpu.VMEM(shape, jnp.bfloat16) for shape in unit_shapes],
            *[pltpu.VMEM(shape, jnp.bfloat16) for shape in unit_shapes],
            *[pltpu.VMEM(shape, jnp.bfloat16) for shape in half_shapes],
            pltpu.VMEM((1, NB), jnp.int32),
            pltpu.VMEM((NB, 3, BP), jnp.float32),
            pltpu.VMEM((NB, BP), jnp.float32),
            pltpu.VMEM((NB, BP), jnp.int32),
            pltpu.VMEM((DEVICES * CAP * 8, BP), jnp.float32),
            pltpu.VMEM((DEVICES, CAP, 8, BP), jnp.bfloat16),
            pltpu.VMEM((DEVICES, CAP, 8, BP), jnp.bfloat16),
            pltpu.VMEM((ROWS, LANES), jnp.float32),
            pltpu.SemaphoreType.DMA((5,)),
            pltpu.SemaphoreType.DMA,
            pltpu.SemaphoreType.DMA((N_GX,)),
            pltpu.SemaphoreType.DMA((2, len(UNITS))),
            pltpu.SemaphoreType.DMA((2, len(UNITS))),
        ],
        compiler_params=pltpu.CompilerParams(
            has_side_effects=True, collective_id=0, vmem_limit_bytes=28 << 20
        ),
        name="exchange",
    )(
        *[
            pltpu.with_memory_space_constraint(array, pltpu.HBM)
            for array in (
                owners.reshape(1, NB),
                jnp.transpose(offsets.reshape(3, NB, BP), (1, 0, 2)),
                weights.reshape(NB, BP),
                cells.reshape(NB, BP),
                table,
            )
        ]
    )
    return pl.pallas_call(
        lines_kernel,
        out_shape=jax.ShapeDtypeStruct((2, 6, CX, CY, NZ), jnp.float32),
        in_specs=[VMEM] * (1 + len(UNITS)),
        out_specs=HBM,
        scratch_shapes=[
            pltpu.VMEM((2, 6, CX, CY, NZ), jnp.float32),
            pltpu.SemaphoreType.DMA,
        ],
        compiler_params=pltpu.CompilerParams(vmem_limit_bytes=8 << 20),
        name="lines",
    )(matrix, *parts)


def solution(mesh):
    table = line_table()
    placed = (P(None, ("gx", "gy")), P(("gx", "gy")), P(("gx", "gy"), None), P(("gx", "gy")))
    mapped = jax.shard_map(
        shards,
        mesh=mesh,
        in_specs=(P(),) + placed,
        out_specs=P(None, None, "gx", "gy", None),
        check_vma=False,
    )
    return functools.partial(mapped, jnp.asarray(table))
```

```python
import functools
import math

import jax
import jax.numpy as jnp
import numpy as np
from jax import lax
from jax.experimental import pallas as pl
from jax.experimental.pallas import tpu as pltpu
from jax.sharding import PartitionSpec as P

CX = 8
CY = 64
NZ = 128
BP = 128
CAP = 2
NB = 128
N_GX = 8
N_GY = 16
DEVICES = N_GX * N_GY
ROWS = CX * CY
LANES = 2 * NZ
GRANULE = 16
HALF = ROWS // 2
UNITS = ((0, 0, ROWS), (1, 0, HALF), (1, HALF, HALF), (2, 0, HALF), (2, HALF, HALF))
MESH = pl.DeviceIdType.MESH
ANY = pl.BlockSpec(memory_space=pl.ANY)
HBM = pl.BlockSpec(memory_space=pltpu.HBM)
VMEM = pl.BlockSpec(memory_space=pltpu.VMEM)


def granules(unit):
    return unit[2] // (N_GY * GRANULE)


def reversed4(value):
    return value % 2 * 8 + value // 2 % 2 * 4 + value // 4 % 2 * 2 + value // 8


def real_transform(values):
    count = len(values)
    if count == 2:
        return [(values[0] + values[1], None), (values[0] - values[1], None)]
    even = real_transform(values[::2])
    odd = real_transform(values[1::2])
    half = count // 2

    def at(spectrum, k):
        if k <= half // 2:
            return spectrum[k]
        re, im = spectrum[half - k]
        return re, None if im is None else -im

    result = []
    for k in range(half + 1):
        ere, eim = at(even, k % half)
        ore, oim = at(odd, k % half)
        if k == 0 or k == half:
            pre, pim = (ore, oim) if k == 0 else (-ore, None if oim is None else -oim)
        elif 4 * k == count:
            pre, pim = (oim, -ore)
        else:
            angle = 2.0 * math.pi * k / count
            cos, sin = math.cos(angle), math.sin(angle)
            if oim is None:
                pre, pim = ore * cos, ore * -sin
            else:
                pre, pim = ore * cos + oim * sin, oim * cos - ore * sin

        def plus(u, v):
            return v if u is None else u if v is None else u + v

        result.append((plus(ere, pre), plus(eim, pim)))
    return result


def write_slots(owner, offsets, weights, cells, planes, send_ref):
    a, b, c = (offsets[:, i, :] for i in range(3))
    scaled = weights / jnp.maximum(a * a + b * b + c * c, 0.25)
    pairs = ((a, a), (b, b), (c, c), (a, b), (b, c), (c, a))
    values = [(first * second * scaled).astype(jnp.bfloat16) for first, second in pairs]
    row = (cells >> 7) - ROWS // 2
    values += [code.astype(jnp.float32).astype(jnp.bfloat16) for code in (row, cells & (NZ - 1))]
    across = jnp.broadcast_to(owner.astype(jnp.float32), (NB, NB))
    same = jnp.where(across == across.T, 1.0, 0.0)
    block = lax.broadcasted_iota(jnp.int32, (NB, NB), 0)
    before = jnp.where(block < lax.broadcasted_iota(jnp.int32, (NB, NB), 1), same, 0.0)
    slot = owner.astype(jnp.float32) * CAP + jnp.sum(before, axis=0, keepdims=True)
    slots = lax.broadcasted_iota(jnp.int32, (DEVICES * CAP, NB), 0).astype(jnp.float32)
    hot = jnp.where(slots == slot, 1.0, 0.0).astype(jnp.bfloat16)
    for k, value in enumerate(values):
        placed = jnp.dot(hot, value, preferred_element_type=jnp.float32)
        planes[pl.ds(k, DEVICES * CAP, stride=8), :] = placed
    send_ref[...] = planes[...].reshape(DEVICES, CAP, 8, BP).astype(jnp.bfloat16)


def exchange_kernel(owner_hbm, offset_hbm, weight_hbm, cell_hbm, table_hbm, *refs):
    count = len(UNITS)
    outs, refs = refs[:count], refs[count:]
    matrix_ref, refs = refs[0], refs[1:]
    fields, refs = refs[:count], refs[count:]
    gathered, refs = refs[:count], refs[count:]
    partials, refs = refs[:count], refs[count:]
    owner_ref, offset_ref, weight_ref, cell_ref, planes, send_ref, recv, acc = refs[:8]
    load_sems, route_send, route_recv, sends, recvs = refs[8:]
    gx = lax.axis_index("gx")
    gy = lax.axis_index("gy")
    me = gx * N_GY + gy

    loads = [
        pltpu.make_async_copy(source, target, load_sems.at[i])
        for i, (source, target) in enumerate(
            (
                (owner_hbm, owner_ref),
                (offset_hbm, offset_ref),
                (weight_hbm, weight_ref),
                (cell_hbm, cell_ref),
            )
        )
    ]
    for load in loads:
        load.start()
    matrix_load = pltpu.make_async_copy(
        table_hbm.at[reversed4(gy)], matrix_ref, load_sems.at[len(loads)]
    )
    matrix_load.start()
    barrier = pltpu.get_barrier_semaphore()

    peers_y = [gy] + [lax.rem(gy + i, N_GY) for i in range(1, N_GY)]

    def greet(j, carry):
        to_x = lax.rem(gx + j, N_GX)
        for to_y in peers_y:
            pl.semaphore_signal(barrier, inc=1, device_id=(to_x, to_y), device_id_type=MESH)
        return carry

    for to_y in peers_y[1:]:
        pl.semaphore_signal(barrier, inc=1, device_id=(gx, to_y), device_id_type=MESH)
    lax.fori_loop(1, N_GX, greet, 0)
    for load in loads:
        load.wait()
    write_slots(owner_ref[...], offset_ref, weight_ref[...], cell_ref[...], planes, send_ref)
    pl.semaphore_wait(barrier, DEVICES - 1)

    pltpu.make_async_copy(send_ref.at[me], recv.at[me], route_recv.at[0]).start()

    def route(j, to_x, peers):
        for to_y in peers:
            pltpu.make_async_remote_copy(
                src_ref=send_ref.at[to_x * N_GY + to_y],
                dst_ref=recv.at[me],
                send_sem=route_send,
                recv_sem=route_recv.at[j],
                device_id=(to_x, to_y),
                device_id_type=MESH,
            ).start()

    def route_step(j, carry):
        route(j, lax.rem(gx + j, N_GX), peers_y)
        return carry

    route(0, gx, peers_y[1:])
    lax.fori_loop(1, N_GX, route_step, 0)

    depth_index = lax.broadcasted_iota(jnp.int32, (NZ, BP), 0)
    depth_index = depth_index.astype(jnp.float32).astype(jnp.bfloat16)
    one_value = jnp.ones((), jnp.bfloat16)
    zero_value = jnp.zeros((), jnp.bfloat16)

    def deposit(pair, low, rows, first, phases):
        row_index = lax.broadcasted_iota(jnp.int32, (rows, BP), 0) + (low - ROWS // 2)
        row_index = row_index.astype(jnp.float32).astype(jnp.bfloat16)
        row_hot, spread = [], []
        for phase in range(phases):
            base = lax.rem(gx + N_GX - (first + phase), N_GX) * N_GY
            for slot in range(N_GY * CAP):
                block = recv[base + slot // CAP, slot % CAP]
                row = jnp.broadcast_to(block[6:7], (rows, BP))
                depth = jnp.broadcast_to(block[7:8], (NZ, BP)) == depth_index
                row_hot.append(jnp.where(row == row_index, one_value, zero_value))
                terms = [
                    jnp.where(depth, jnp.broadcast_to(block[k : k + 1], (NZ, BP)), zero_value)
                    for k in (2 * pair, 2 * pair + 1)
                ]
                spread.append(jnp.concatenate(terms, axis=0))
        acc[low : low + rows] += lax.dot_general(
            jnp.concatenate(row_hot, axis=1),
            jnp.concatenate(spread, axis=1),
            (((1,), (1,)), ((), ())),
            preferred_element_type=jnp.float32,
        )

    def to_peers(sources, target, slot_of, stage, unit_index):
        pltpu.make_async_copy(
            sources.at[slot_of(gy)], target.at[gy], recvs.at[stage, unit_index]
        ).start()

        for to_y in peers_y[1:]:
            pltpu.make_async_remote_copy(
                src_ref=sources.at[slot_of(to_y)],
                dst_ref=target.at[gy],
                send_sem=sends.at[stage, unit_index],
                recv_sem=recvs.at[stage, unit_index],
                device_id=(gx, to_y),
                device_id_type=MESH,
            ).start()

    def scatter_fields(u):
        parts = granules(UNITS[u])
        for i in range(N_GY):
            for g in range(parts):
                start = UNITS[u][1] + (i * parts + g) * GRANULE
                fields[u][i, g] = acc[start : start + GRANULE].astype(jnp.bfloat16)
        to_peers(fields[u], gathered[u], lambda device: device, 0, u)

    def frequency_slot(device):
        rem, div = lax.rem, lax.div
        freq = rem(device, 2) * 8 + rem(div(device, 2), 2) * 4
        freq = freq + rem(div(device, 4), 2) * 2 + div(device, 8)
        return 8 - (freq - 8) * (2 * div(freq, 8) - 1)

    def transform(u):
        pltpu.make_async_copy(gathered[u], gathered[u], recvs.at[0, u]).wait()
        for g in range(granules(UNITS[u])):
            for half in range(LANES // 128):
                lanes = slice(128 * half, 128 * half + 128)
                values = [gathered[u][s, g, :, lanes].astype(jnp.float32) for s in range(N_GY)]
                for r, (re, im) in enumerate(real_transform(values)):
                    im = jnp.zeros_like(re) if im is None else im
                    partials[u][r, g, 0, :, lanes] = re.astype(jnp.bfloat16)
                    partials[u][r, g, 1, :, lanes] = im.astype(jnp.bfloat16)
        to_peers(partials[u], outs[u], frequency_slot, 1, u)

    def run(pair, low, rows, first, last, phases, arriving=False):
        def step(i, carry):
            for phase in range(phases if arriving else 0):
                arrived = recv.at[pl.ds(0, N_GY)]
                sem = route_recv.at[i * phases + phase]
                pltpu.make_async_copy(arrived, arrived, sem).wait()
            deposit(pair, low, rows, i * phases, phases)
            return carry

        lax.fori_loop(first // phases, last // phases, step, 0)

    acc[...] = jnp.zeros_like(acc)
    run(0, 0, ROWS, 0, 2, 1, arriving=True)
    run(0, 0, ROWS, 2, N_GX, 2, arriving=True)
    scatter_fields(0)
    acc[...] = jnp.zeros_like(acc)
    run(1, 0, HALF, 0, N_GX, 4)
    scatter_fields(1)
    run(1, HALF, HALF, 0, N_GX // 2, 2)
    transform(0)
    run(1, HALF, HALF, N_GX // 2, N_GX, 2)
    scatter_fields(2)
    transform(1)
    acc[...] = jnp.zeros_like(acc)
    run(2, 0, HALF, 0, N_GX, 4)
    scatter_fields(3)
    run(2, HALF, HALF, 0, N_GX - 2, 2)
    transform(2)
    run(2, HALF, HALF, N_GX - 2, N_GX, 2)
    scatter_fields(4)
    transform(3)
    transform(4)
    matrix_load.wait()

    sent = send_ref.at[pl.ds(0, DEVICES - 1)]
    pltpu.make_async_copy(sent, sent, route_send).wait()
    for u in range(count):
        sent = fields[u].at[pl.ds(0, N_GY - 1)]
        pltpu.make_async_copy(sent, sent, sends.at[0, u]).wait()
        sent = outs[u].at[pl.ds(0, N_GY - 1)]
        pltpu.make_async_copy(sent, sent, sends.at[1, u]).wait()
        pltpu.make_async_copy(outs[u], outs[u], recvs.at[1, u]).wait()


def lines_kernel(matrix, *refs):
    parts, (out_ref, staged, store_sem) = refs[: len(UNITS)], refs[len(UNITS) :]
    for u, (pair, low, rows) in enumerate(UNITS):
        sources = N_GY * CY // rows
        for x in range(rows // CY):
            values = parts[u][sources * x : sources * x + sources].reshape(2 * CY, LANES)
            lines = jnp.dot(matrix[0], values, preferred_element_type=jnp.float32)
            lines += jnp.dot(matrix[1], values, preferred_element_type=jnp.float32)
            to_x = low // CY + x
            for half in range(2):
                for k in range(2):
                    staged[half, 2 * pair + k, to_x] = lines[
                        half * CY : half * CY + CY, k * NZ : k * NZ + NZ
                    ]
            if x % 4 == 3:
                for half in range(2):
                    at = (half, pl.ds(2 * pair, 2), pl.ds(to_x - 3, 4))
                    pltpu.make_async_copy(staged.at[at], out_ref.at[at], store_sem).start()
    pltpu.make_async_copy(staged, out_ref, store_sem).wait()


def line_table():
    y = np.arange(CY)
    q = np.arange(CY)
    tables = []
    for freq in range(N_GY):
        phase = (q[:, None] * N_GY + freq) * y[None, :] % (CY * N_GY)
        angle = phase * (2.0 * np.pi / (CY * N_GY))
        cos, sin = np.cos(angle), np.sin(angle)
        sign = -1.0 if freq > N_GY // 2 else 1.0
        full = np.stack([np.stack([cos, sign * sin], 1), np.stack([-sin, sign * cos], 1)])
        full = full.reshape(2, CY, 2, CY // GRANULE, GRANULE).transpose(0, 1, 3, 2, 4)
        full = full.reshape(2 * CY, 2 * CY)
        high = full.astype(jnp.bfloat16)
        tables.append(np.stack([high, (full - high.astype(np.float64)).astype(jnp.bfloat16)]))
    return np.stack(tables)


def shards(table, offsets, weights, owners, cells):
    unit_shapes = [(N_GY, granules(unit), GRANULE, LANES) for unit in UNITS]
    half_shapes = [(9, granules(unit), 2, GRANULE, LANES) for unit in UNITS]
    out_shapes = [(N_GY, granules(unit), 2, GRANULE, LANES) for unit in UNITS]
    *parts, matrix = pl.pallas_call(
        exchange_kernel,
        out_shape=[jax.ShapeDtypeStruct(shape, jnp.bfloat16) for shape in out_shapes]
        + [jax.ShapeDtypeStruct((2, 2 * CY, 2 * CY), jnp.bfloat16)],
        in_specs=[HBM] * 5,
        out_specs=[ANY] * (1 + len(UNITS)),
        scratch_shapes=[
            *[pltpu.VMEM(shape, jnp.bfloat16) for shape in unit_shapes],
            *[pltpu.VMEM(shape, jnp.bfloat16) for shape in unit_shapes],
            *[pltpu.VMEM(shape, jnp.bfloat16) for shape in half_shapes],
            pltpu.VMEM((1, NB), jnp.int32),
            pltpu.VMEM((NB, 3, BP), jnp.float32),
            pltpu.VMEM((NB, BP), jnp.float32),
            pltpu.VMEM((NB, BP), jnp.int32),
            pltpu.VMEM((DEVICES * CAP * 8, BP), jnp.float32),
            pltpu.VMEM((DEVICES, CAP, 8, BP), jnp.bfloat16),
            pltpu.VMEM((DEVICES, CAP, 8, BP), jnp.bfloat16),
            pltpu.VMEM((ROWS, LANES), jnp.float32),
            pltpu.SemaphoreType.DMA((5,)),
            pltpu.SemaphoreType.DMA,
            pltpu.SemaphoreType.DMA((N_GX,)),
            pltpu.SemaphoreType.DMA((2, len(UNITS))),
            pltpu.SemaphoreType.DMA((2, len(UNITS))),
        ],
        compiler_params=pltpu.CompilerParams(
            has_side_effects=True, collective_id=0, vmem_limit_bytes=48 << 20
        ),
        name="exchange",
    )(
        *[
            pltpu.with_memory_space_constraint(array, pltpu.HBM)
            for array in (
                owners.reshape(1, NB),
                jnp.transpose(offsets.reshape(3, NB, BP), (1, 0, 2)),
                weights.reshape(NB, BP),
                cells.reshape(NB, BP),
                table,
            )
        ]
    )
    return pl.pallas_call(
        lines_kernel,
        out_shape=jax.ShapeDtypeStruct((2, 6, CX, CY, NZ), jnp.float32),
        in_specs=[VMEM] * (1 + len(UNITS)),
        out_specs=HBM,
        scratch_shapes=[
            pltpu.VMEM((2, 6, CX, CY, NZ), jnp.float32),
            pltpu.SemaphoreType.DMA,
        ],
        compiler_params=pltpu.CompilerParams(vmem_limit_bytes=8 << 20),
        name="lines",
    )(matrix, *parts)


def solution(mesh):
    table = line_table()
    placed = (P(None, ("gx", "gy")), P(("gx", "gy")), P(("gx", "gy"), None), P(("gx", "gy")))
    mapped = jax.shard_map(
        shards,
        mesh=mesh,
        in_specs=(P(),) + placed,
        out_specs=P(None, None, "gx", "gy", None),
        check_vma=False,
    )
    return functools.partial(mapped, jnp.asarray(table))
```

```python
import functools
import math

import jax
import jax.numpy as jnp
import numpy as np
from jax import lax
from jax.experimental import pallas as pl
from jax.experimental.pallas import tpu as pltpu
from jax.sharding import PartitionSpec as P

CX = 8
CY = 64
NZ = 128
BP = 128
CAP = 2
NB = 128
N_GX = 8
N_GY = 16
DEVICES = N_GX * N_GY
ROWS = CX * CY
LANES = 2 * NZ
GRANULE = 16
HALF = ROWS // 2
UNITS = ((0, 0, ROWS), (1, 0, HALF), (1, HALF, HALF), (2, 0, HALF), (2, HALF, HALF))
MESH = pl.DeviceIdType.MESH
ANY = pl.BlockSpec(memory_space=pl.ANY)
HBM = pl.BlockSpec(memory_space=pltpu.HBM)
VMEM = pl.BlockSpec(memory_space=pltpu.VMEM)


def granules(unit):
    return unit[2] // (N_GY * GRANULE)


def hops(offset):
    return sum(min(step, 4 - step) for step in offset)


def offsets_by_distance(with_z):
    span = range(4) if with_z else range(1)
    cores = range(2) if with_z else range(1)
    every = [(z, c, y, x) for z in span for c in cores for y in range(4) for x in range(4)]
    return sorted(every, key=lambda o: (hops((o[0], o[2], o[3])), o[1]))


ROUTE = offsets_by_distance(True)
PLANE = offsets_by_distance(False)


def reversed4(value):
    return value % 2 * 8 + value // 2 % 2 * 4 + value // 4 % 2 * 2 + value // 8


def real_transform(values):
    count = len(values)
    if count == 2:
        return [(values[0] + values[1], None), (values[0] - values[1], None)]
    even = real_transform(values[::2])
    odd = real_transform(values[1::2])
    half = count // 2

    def at(spectrum, k):
        if k <= half // 2:
            return spectrum[k]
        re, im = spectrum[half - k]
        return re, None if im is None else -im

    result = []
    for k in range(half + 1):
        ere, eim = at(even, k % half)
        ore, oim = at(odd, k % half)
        if k == 0 or k == half:
            pre, pim = (ore, oim) if k == 0 else (-ore, None if oim is None else -oim)
        elif 4 * k == count:
            pre, pim = (oim, -ore)
        else:
            angle = 2.0 * math.pi * k / count
            cos, sin = math.cos(angle), math.sin(angle)
            if oim is None:
                pre, pim = ore * cos, ore * -sin
            else:
                pre, pim = ore * cos + oim * sin, oim * cos - ore * sin

        def plus(u, v):
            return v if u is None else u if v is None else u + v

        result.append((plus(ere, pre), plus(eim, pim)))
    return result


def write_slots(owner, offsets, weights, cells, planes, send_ref):
    a, b, c = (offsets[:, i, :] for i in range(3))
    scaled = weights / jnp.maximum(a * a + b * b + c * c, 0.25)
    pairs = ((a, a), (b, b), (c, c), (a, b), (b, c), (c, a))
    values = [(first * second * scaled).astype(jnp.bfloat16) for first, second in pairs]
    row = (cells >> 7) - ROWS // 2
    values += [code.astype(jnp.float32).astype(jnp.bfloat16) for code in (row, cells & (NZ - 1))]
    across = jnp.broadcast_to(owner.astype(jnp.float32), (NB, NB))
    same = jnp.where(across == across.T, 1.0, 0.0)
    block = lax.broadcasted_iota(jnp.int32, (NB, NB), 0)
    before = jnp.where(block < lax.broadcasted_iota(jnp.int32, (NB, NB), 1), same, 0.0)
    slot = owner.astype(jnp.float32) * CAP + jnp.sum(before, axis=0, keepdims=True)
    slots = lax.broadcasted_iota(jnp.int32, (DEVICES * CAP, NB), 0).astype(jnp.float32)
    hot = jnp.where(slots == slot, 1.0, 0.0).astype(jnp.bfloat16)
    for k, value in enumerate(values):
        placed = jnp.dot(hot, value, preferred_element_type=jnp.float32)
        planes[pl.ds(k, DEVICES * CAP, stride=8), :] = placed
    send_ref[...] = planes[...].reshape(DEVICES, CAP, 8, BP).astype(jnp.bfloat16)


def unit_lines(unit, matrix, part, target, first_k, first_x):
    sources = N_GY * CY // unit[2]
    for x in range(unit[2] // CY):
        values = part[sources * x : sources * x + sources].reshape(2 * CY, LANES)
        lines = jnp.dot(matrix[0], values, preferred_element_type=jnp.float32)
        lines += jnp.dot(matrix[1], values, preferred_element_type=jnp.float32)
        for half in range(2):
            for k in range(2):
                target[half, first_k + k, first_x + x] = lines[
                    half * CY : half * CY + CY, k * NZ : k * NZ + NZ
                ]


def exchange_kernel(owner_hbm, offset_hbm, weight_hbm, cell_hbm, table_hbm, *refs):
    count = len(UNITS)
    (last_ref, matrix_ref, done_ref), refs = refs[:3], refs[3:]
    outs, refs = (*refs[: count - 1], last_ref), refs[count - 1 :]
    fields, refs = refs[:count], refs[count:]
    gathered, refs = refs[:count], refs[count:]
    partials, refs = refs[:count], refs[count:]
    owner_ref, offset_ref, weight_ref, cell_ref, planes, send_ref, recv, acc = refs[:8]
    matrix, staged, load_sems, route_send, route_recv, sends, recvs, done_sems = refs[8:]
    gx = lax.axis_index("gx")
    gy = lax.axis_index("gy")
    me = gx * N_GY + gy

    loads = [
        pltpu.make_async_copy(source, target, load_sems.at[i])
        for i, (source, target) in enumerate(
            (
                (owner_hbm, owner_ref),
                (offset_hbm, offset_ref),
                (weight_hbm, weight_ref),
                (cell_hbm, cell_ref),
            )
        )
    ]
    for load in loads:
        load.start()
    matrix_load = pltpu.make_async_copy(
        table_hbm.at[reversed4(gy)], matrix_ref, load_sems.at[len(loads)]
    )
    matrix_load.start()
    own_load = pltpu.make_async_copy(table_hbm.at[reversed4(gy)], matrix, load_sems.at[5])
    own_load.start()
    barrier = pltpu.get_barrier_semaphore()

    rem, div = lax.rem, lax.div
    columns = {
        (z, c): rem(div(gx, 2) + z, 4) * 2 + rem(gx + c, 2) for z in range(4) for c in range(2)
    }
    places = {
        (y, x): rem(div(gy, 4) + y, 4) * 4 + rem(gy + x, 4) for y in range(4) for x in range(4)
    }
    routes = [(columns[offset[:2]], places[offset[2:]]) for offset in ROUTE]
    peers = [places[offset[2:]] for offset in PLANE[1:]]
    for device in routes[:0:-1]:
        pl.semaphore_signal(barrier, inc=1, device_id=device, device_id_type=MESH)
    for load in loads:
        load.wait()
    write_slots(owner_ref[...], offset_ref, weight_ref[...], cell_ref[...], planes, send_ref)
    pl.semaphore_wait(barrier, DEVICES - 1)

    pltpu.make_async_copy(send_ref.at[me], recv.at[0], route_recv.at[0]).start()
    for i, device in enumerate(routes):
        if i:
            pltpu.make_async_remote_copy(
                src_ref=send_ref.at[device[0] * N_GY + device[1]],
                dst_ref=recv.at[i],
                send_sem=route_send,
                recv_sem=route_recv.at[i // N_GY],
                device_id=device,
                device_id_type=MESH,
            ).start()

    depth_index = lax.broadcasted_iota(jnp.int32, (NZ, BP), 0)
    depth_index = depth_index.astype(jnp.float32).astype(jnp.bfloat16)
    one_value = jnp.ones((), jnp.bfloat16)
    zero_value = jnp.zeros((), jnp.bfloat16)

    def deposit(pair, low, rows, first, phases):
        row_index = lax.broadcasted_iota(jnp.int32, (rows, BP), 0) + (low - ROWS // 2)
        row_index = row_index.astype(jnp.float32).astype(jnp.bfloat16)
        row_hot, spread = [], []
        for phase in range(phases):
            base = (first + phase) * N_GY
            for slot in range(N_GY * CAP):
                block = recv[base + slot // CAP, slot % CAP]
                row = jnp.broadcast_to(block[6:7], (rows, BP))
                depth = jnp.broadcast_to(block[7:8], (NZ, BP)) == depth_index
                row_hot.append(jnp.where(row == row_index, one_value, zero_value))
                terms = [
                    jnp.where(depth, jnp.broadcast_to(block[k : k + 1], (NZ, BP)), zero_value)
                    for k in (2 * pair, 2 * pair + 1)
                ]
                spread.append(jnp.concatenate(terms, axis=0))
        acc[low : low + rows] += lax.dot_general(
            jnp.concatenate(row_hot, axis=1),
            jnp.concatenate(spread, axis=1),
            (((1,), (1,)), ((), ())),
            preferred_element_type=jnp.float32,
        )

    def to_peers(sources, target, slot_of, stage, unit_index):
        pltpu.make_async_copy(
            sources.at[slot_of(gy)], target.at[gy], recvs.at[stage, unit_index]
        ).start()

        for to_y in peers:
            pltpu.make_async_remote_copy(
                src_ref=sources.at[slot_of(to_y)],
                dst_ref=target.at[gy],
                send_sem=sends.at[stage, unit_index],
                recv_sem=recvs.at[stage, unit_index],
                device_id=(gx, to_y),
                device_id_type=MESH,
            ).start()

    def scatter_fields(u):
        parts = granules(UNITS[u])
        for i in range(N_GY):
            for g in range(parts):
                start = UNITS[u][1] + (i * parts + g) * GRANULE
                fields[u][i, g] = acc[start : start + GRANULE].astype(jnp.bfloat16)
        to_peers(fields[u], gathered[u], lambda device: device, 0, u)

    def frequency_slot(device):
        freq = rem(device, 2) * 8 + rem(div(device, 2), 2) * 4
        freq = freq + rem(div(device, 4), 2) * 2 + div(device, 8)
        return 8 - (freq - 8) * (2 * div(freq, 8) - 1)

    def transform(u):
        pltpu.make_async_copy(gathered[u], gathered[u], recvs.at[0, u]).wait()
        for g in range(granules(UNITS[u])):
            for half in range(LANES // 128):
                lanes = slice(128 * half, 128 * half + 128)
                values = [gathered[u][s, g, :, lanes].astype(jnp.float32) for s in range(N_GY)]
                for r, (re, im) in enumerate(real_transform(values)):
                    im = jnp.zeros_like(re) if im is None else im
                    partials[u][r, g, 0, :, lanes] = re.astype(jnp.bfloat16)
                    partials[u][r, g, 1, :, lanes] = im.astype(jnp.bfloat16)
        to_peers(partials[u], outs[u], frequency_slot, 1, u)

    def run(pair, low, rows, first, last, phases, arriving=False, between=None):
        def step(i, carry):
            if between is not None:

                @pl.when(i == between[0])
                def _():
                    transform(between[1])

            for phase in range(phases if arriving else 0):
                arrived = recv.at[pl.ds(0, N_GY)]
                sem = route_recv.at[i * phases + phase]
                pltpu.make_async_copy(arrived, arrived, sem).wait()
            deposit(pair, low, rows, i * phases, phases)
            return carry

        lax.fori_loop(first // phases, last // phases, step, 0)

    acc[...] = jnp.zeros_like(acc)
    run(0, 0, ROWS, 0, 2, 1, arriving=True)
    run(0, 0, ROWS, 2, N_GX, 2, arriving=True)
    scatter_fields(0)
    acc[...] = jnp.zeros_like(acc)
    run(1, 0, HALF, 0, N_GX, 4)
    scatter_fields(1)
    run(1, HALF, HALF, 0, N_GX, 2, between=(2, 0))
    scatter_fields(2)
    transform(1)
    acc[...] = jnp.zeros_like(acc)
    run(2, 0, HALF, 0, N_GX, 4)
    scatter_fields(3)
    transform(2)
    run(2, HALF, HALF, 0, N_GX, 2, between=(3, 3))
    scatter_fields(4)

    def finish(u):
        pltpu.make_async_copy(outs[u], outs[u], recvs.at[1, u]).wait()
        pair, low, rows = UNITS[u]
        unit_lines(UNITS[u], matrix, outs[u], staged, 2 * pair, low // CY)
        for half in range(2):
            at = (half, pl.ds(2 * pair, 2), pl.ds(low // CY, rows // CY))
            copy = pltpu.make_async_copy(staged.at[at], done_ref.at[at], done_sems.at[u, half])
            copy.start()
            moved.append(copy)

    moved = [matrix_load]
    own_load.wait()
    finish(0)
    finish(1)
    transform(4)
    finish(2)
    finish(3)
    for copy in moved:
        copy.wait()

    sent = send_ref.at[pl.ds(0, DEVICES - 1)]
    pltpu.make_async_copy(sent, sent, route_send).wait()
    for u in range(count):
        sent = fields[u].at[pl.ds(0, N_GY - 1)]
        pltpu.make_async_copy(sent, sent, sends.at[0, u]).wait()
        sent = outs[u].at[pl.ds(0, N_GY - 1)]
        pltpu.make_async_copy(sent, sent, sends.at[1, u]).wait()
    pltpu.make_async_copy(outs[4], outs[4], recvs.at[1, 4]).wait()


def lines_kernel(matrix, part, done_ref, out_ref, last, sems):
    pair, low, rows = UNITS[-1]
    copies = []
    for half in range(2):
        for u in range(len(UNITS) - 1):
            at = (half, pl.ds(2 * UNITS[u][0], 2), pl.ds(UNITS[u][1] // CY, UNITS[u][2] // CY))
            copies.append((done_ref.at[at], out_ref.at[at]))
    for i, (source, target) in enumerate(copies):
        pltpu.make_async_copy(source, target, sems.at[i]).start()
    unit_lines(UNITS[-1], matrix, part, last, 0, 0)
    for half in range(2):
        at = (half, pl.ds(2 * pair, 2), pl.ds(low // CY, rows // CY))
        copies.append((last.at[half], out_ref.at[at]))
        i = len(copies) - 1
        pltpu.make_async_copy(*copies[i], sems.at[i]).start()
    for i, (source, target) in enumerate(copies):
        pltpu.make_async_copy(source, target, sems.at[i]).wait()


def line_table():
    y = np.arange(CY)
    q = np.arange(CY)
    tables = []
    for freq in range(N_GY):
        phase = (q[:, None] * N_GY + freq) * y[None, :] % (CY * N_GY)
        angle = phase * (2.0 * np.pi / (CY * N_GY))
        cos, sin = np.cos(angle), np.sin(angle)
        sign = -1.0 if freq > N_GY // 2 else 1.0
        full = np.stack([np.stack([cos, sign * sin], 1), np.stack([-sin, sign * cos], 1)])
        full = full.reshape(2, CY, 2, CY // GRANULE, GRANULE).transpose(0, 1, 3, 2, 4)
        full = full.reshape(2 * CY, 2 * CY)
        high = full.astype(jnp.bfloat16)
        tables.append(np.stack([high, (full - high.astype(np.float64)).astype(jnp.bfloat16)]))
    return np.stack(tables)


def shards(table, offsets, weights, owners, cells):
    unit_shapes = [(N_GY, granules(unit), GRANULE, LANES) for unit in UNITS]
    half_shapes = [(9, granules(unit), 2, GRANULE, LANES) for unit in UNITS]
    out_shapes = [(N_GY, granules(unit), 2, GRANULE, LANES) for unit in UNITS]
    part, matrix, done = pl.pallas_call(
        exchange_kernel,
        out_shape=[
            jax.ShapeDtypeStruct(out_shapes[-1], jnp.bfloat16),
            jax.ShapeDtypeStruct((2, 2 * CY, 2 * CY), jnp.bfloat16),
            jax.ShapeDtypeStruct((2, 6, CX, CY, NZ), jnp.float32),
        ],
        in_specs=[HBM] * 5,
        out_specs=[ANY] * 3,
        scratch_shapes=[
            *[pltpu.VMEM(shape, jnp.bfloat16) for shape in out_shapes[:-1]],
            *[pltpu.VMEM(shape, jnp.bfloat16) for shape in unit_shapes],
            *[pltpu.VMEM(shape, jnp.bfloat16) for shape in unit_shapes],
            *[pltpu.VMEM(shape, jnp.bfloat16) for shape in half_shapes],
            pltpu.VMEM((1, NB), jnp.int32),
            pltpu.VMEM((NB, 3, BP), jnp.float32),
            pltpu.VMEM((NB, BP), jnp.float32),
            pltpu.VMEM((NB, BP), jnp.int32),
            pltpu.VMEM((DEVICES * CAP * 8, BP), jnp.float32),
            pltpu.VMEM((DEVICES, CAP, 8, BP), jnp.bfloat16),
            pltpu.VMEM((DEVICES, CAP, 8, BP), jnp.bfloat16),
            pltpu.VMEM((ROWS, LANES), jnp.float32),
            pltpu.VMEM((2, 2 * CY, 2 * CY), jnp.bfloat16),
            pltpu.VMEM((2, 6, CX, CY, NZ), jnp.float32),
            pltpu.SemaphoreType.DMA((6,)),
            pltpu.SemaphoreType.DMA,
            pltpu.SemaphoreType.DMA((N_GX,)),
            pltpu.SemaphoreType.DMA((2, len(UNITS))),
            pltpu.SemaphoreType.DMA((2, len(UNITS))),
            pltpu.SemaphoreType.DMA((len(UNITS) - 1, 2)),
        ],
        compiler_params=pltpu.CompilerParams(
            has_side_effects=True, collective_id=0, vmem_limit_bytes=48 << 20
        ),
        name="exchange",
    )(
        *[
            pltpu.with_memory_space_constraint(array, pltpu.HBM)
            for array in (
                owners.reshape(1, NB),
                jnp.transpose(offsets.reshape(3, NB, BP), (1, 0, 2)),
                weights.reshape(NB, BP),
                cells.reshape(NB, BP),
                table,
            )
        ]
    )
    return pl.pallas_call(
        lines_kernel,
        out_shape=jax.ShapeDtypeStruct((2, 6, CX, CY, NZ), jnp.float32),
        in_specs=[VMEM] * 3,
        out_specs=HBM,
        scratch_shapes=[
            pltpu.VMEM((2, 2, UNITS[-1][2] // CY, CY, NZ), jnp.float32),
            pltpu.SemaphoreType.DMA((2 * len(UNITS),)),
        ],
        compiler_params=pltpu.CompilerParams(vmem_limit_bytes=8 << 20),
        name="lines",
    )(matrix, part, done)


def solution(mesh):
    table = line_table()
    placed = (P(None, ("gx", "gy")), P(("gx", "gy")), P(("gx", "gy"), None), P(("gx", "gy")))
    mapped = jax.shard_map(
        shards,
        mesh=mesh,
        in_specs=(P(),) + placed,
        out_specs=P(None, None, "gx", "gy", None),
        check_vma=False,
    )
    return functools.partial(mapped, jnp.asarray(table))
```

```python
import functools
import math

import jax
import jax.numpy as jnp
import numpy as np
from jax import lax
from jax.experimental import pallas as pl
from jax.experimental.pallas import tpu as pltpu
from jax.sharding import PartitionSpec as P

CX = 8
CY = 64
NZ = 128
BP = 128
CAP = 2
NB = 128
N_GX = 8
N_GY = 16
DEVICES = N_GX * N_GY
ROWS = CX * CY
LANES = 2 * NZ
GRANULE = 16
HALF = ROWS // 2
UNITS = tuple((pair, low, HALF) for pair in range(3) for low in (0, HALF))
MESH = pl.DeviceIdType.MESH
ANY = pl.BlockSpec(memory_space=pl.ANY)
HBM = pl.BlockSpec(memory_space=pltpu.HBM)
VMEM = pl.BlockSpec(memory_space=pltpu.VMEM)


def granules(unit):
    return unit[2] // (N_GY * GRANULE)


def hops(offset):
    return sum(min(step, 4 - step) for step in offset)


def offsets_by_distance(with_z):
    span = range(4) if with_z else range(1)
    cores = range(2) if with_z else range(1)
    every = [(z, c, y, x) for z in span for c in cores for y in range(4) for x in range(4)]
    return sorted(every, key=lambda o: (hops((o[0], o[2], o[3])), o[1]))


ROUTE = offsets_by_distance(True)
PLANE = offsets_by_distance(False)


def reversed4(value):
    return value % 2 * 8 + value // 2 % 2 * 4 + value // 4 % 2 * 2 + value // 8


def real_transform(values):
    count = len(values)
    if count == 2:
        return [(values[0] + values[1], None), (values[0] - values[1], None)]
    even = real_transform(values[::2])
    odd = real_transform(values[1::2])
    half = count // 2

    def at(spectrum, k):
        if k <= half // 2:
            return spectrum[k]
        re, im = spectrum[half - k]
        return re, None if im is None else -im

    result = []
    for k in range(half + 1):
        ere, eim = at(even, k % half)
        ore, oim = at(odd, k % half)
        if k == 0 or k == half:
            pre, pim = (ore, oim) if k == 0 else (-ore, None if oim is None else -oim)
        elif 4 * k == count:
            pre, pim = (oim, -ore)
        else:
            angle = 2.0 * math.pi * k / count
            cos, sin = math.cos(angle), math.sin(angle)
            if oim is None:
                pre, pim = ore * cos, ore * -sin
            else:
                pre, pim = ore * cos + oim * sin, oim * cos - ore * sin

        def plus(u, v):
            return v if u is None else u if v is None else u + v

        result.append((plus(ere, pre), plus(eim, pim)))
    return result


def write_slots(owner, offsets, weights, cells, planes, send_ref):
    a, b, c = (offsets[:, i, :] for i in range(3))
    scaled = weights / jnp.maximum(a * a + b * b + c * c, 0.25)
    pairs = ((a, a), (b, b), (c, c), (a, b), (b, c), (c, a))
    values = [(first * second * scaled).astype(jnp.bfloat16) for first, second in pairs]
    row = (cells >> 7) - ROWS // 2
    values += [code.astype(jnp.float32).astype(jnp.bfloat16) for code in (row, cells & (NZ - 1))]
    across = jnp.broadcast_to(owner.astype(jnp.float32), (NB, NB))
    same = jnp.where(across == across.T, 1.0, 0.0)
    block = lax.broadcasted_iota(jnp.int32, (NB, NB), 0)
    before = jnp.where(block < lax.broadcasted_iota(jnp.int32, (NB, NB), 1), same, 0.0)
    slot = owner.astype(jnp.float32) * CAP + jnp.sum(before, axis=0, keepdims=True)
    slots = lax.broadcasted_iota(jnp.int32, (DEVICES * CAP, NB), 0).astype(jnp.float32)
    hot = jnp.where(slots == slot, 1.0, 0.0).astype(jnp.bfloat16)
    for k, value in enumerate(values):
        placed = jnp.dot(hot, value, preferred_element_type=jnp.float32)
        planes[pl.ds(k, DEVICES * CAP, stride=8), :] = placed
    send_ref[...] = planes[...].reshape(DEVICES, CAP, 8, BP).astype(jnp.bfloat16)


def unit_lines(unit, matrix, part, target, first_k, first_x):
    sources = N_GY * CY // unit[2]
    for x in range(unit[2] // CY):
        values = part[sources * x : sources * x + sources].reshape(2 * CY, LANES)
        lines = jnp.dot(matrix[0], values, preferred_element_type=jnp.float32)
        lines += jnp.dot(matrix[1], values, preferred_element_type=jnp.float32)
        for half in range(2):
            for k in range(2):
                target[half, first_k + k, first_x + x] = lines[
                    half * CY : half * CY + CY, k * NZ : k * NZ + NZ
                ]


def exchange_kernel(owner_hbm, offset_hbm, weight_hbm, cell_hbm, table_hbm, *refs):
    count = len(UNITS)
    (last_ref, matrix_ref, done_ref), refs = refs[:3], refs[3:]
    outs, refs = (*refs[: count - 1], last_ref), refs[count - 1 :]
    fields, refs = refs[:count], refs[count:]
    gathered, refs = refs[:count], refs[count:]
    partials, refs = refs[:count], refs[count:]
    owner_ref, offset_ref, weight_ref, cell_ref, planes, send_ref, recv, acc = refs[:8]
    matrix, staged, load_sems, route_send, route_recv, sends, recvs, done_sems = refs[8:]
    gx = lax.axis_index("gx")
    gy = lax.axis_index("gy")
    me = gx * N_GY + gy

    loads = [
        pltpu.make_async_copy(source, target, load_sems.at[i])
        for i, (source, target) in enumerate(
            (
                (owner_hbm, owner_ref),
                (offset_hbm, offset_ref),
                (weight_hbm, weight_ref),
                (cell_hbm, cell_ref),
            )
        )
    ]
    for load in loads:
        load.start()
    matrix_load = pltpu.make_async_copy(
        table_hbm.at[reversed4(gy)], matrix_ref, load_sems.at[len(loads)]
    )
    matrix_load.start()
    own_load = pltpu.make_async_copy(table_hbm.at[reversed4(gy)], matrix, load_sems.at[5])
    own_load.start()
    barrier = pltpu.get_barrier_semaphore()

    rem, div = lax.rem, lax.div
    columns = {
        (z, c): rem(div(gx, 2) + z, 4) * 2 + rem(gx + c, 2) for z in range(4) for c in range(2)
    }
    places = {
        (y, x): rem(div(gy, 4) + y, 4) * 4 + rem(gy + x, 4) for y in range(4) for x in range(4)
    }
    routes = [(columns[offset[:2]], places[offset[2:]]) for offset in ROUTE]
    peers = [places[offset[2:]] for offset in PLANE[1:]]
    for device in routes[:0:-1]:
        pl.semaphore_signal(barrier, inc=1, device_id=device, device_id_type=MESH)
    for load in loads:
        load.wait()
    write_slots(owner_ref[...], offset_ref, weight_ref[...], cell_ref[...], planes, send_ref)
    pl.semaphore_wait(barrier, DEVICES - 1)

    pltpu.make_async_copy(send_ref.at[me], recv.at[0], route_recv.at[0]).start()
    for i, device in enumerate(routes):
        if i:
            pltpu.make_async_remote_copy(
                src_ref=send_ref.at[device[0] * N_GY + device[1]],
                dst_ref=recv.at[i],
                send_sem=route_send,
                recv_sem=route_recv.at[i // N_GY],
                device_id=device,
                device_id_type=MESH,
            ).start()

    depth_index = lax.broadcasted_iota(jnp.int32, (NZ, BP), 0)
    depth_index = depth_index.astype(jnp.float32).astype(jnp.bfloat16)
    one_value = jnp.ones((), jnp.bfloat16)
    zero_value = jnp.zeros((), jnp.bfloat16)

    def deposit(pair, low, rows, first, phases):
        row_index = lax.broadcasted_iota(jnp.int32, (rows, BP), 0) + (low - ROWS // 2)
        row_index = row_index.astype(jnp.float32).astype(jnp.bfloat16)
        row_hot, spread = [], []
        for phase in range(phases):
            base = (first + phase) * N_GY
            for slot in range(N_GY * CAP):
                block = recv[base + slot // CAP, slot % CAP]
                row = jnp.broadcast_to(block[6:7], (rows, BP))
                depth = jnp.broadcast_to(block[7:8], (NZ, BP)) == depth_index
                row_hot.append(jnp.where(row == row_index, one_value, zero_value))
                terms = [
                    jnp.where(depth, jnp.broadcast_to(block[k : k + 1], (NZ, BP)), zero_value)
                    for k in (2 * pair, 2 * pair + 1)
                ]
                spread.append(jnp.concatenate(terms, axis=0))
        acc[low : low + rows] += lax.dot_general(
            jnp.concatenate(row_hot, axis=1),
            jnp.concatenate(spread, axis=1),
            (((1,), (1,)), ((), ())),
            preferred_element_type=jnp.float32,
        )

    def to_peers(sources, target, slot_of, stage, unit_index):
        pltpu.make_async_copy(
            sources.at[slot_of(gy)], target.at[gy], recvs.at[stage, unit_index]
        ).start()

        for to_y in peers:
            pltpu.make_async_remote_copy(
                src_ref=sources.at[slot_of(to_y)],
                dst_ref=target.at[gy],
                send_sem=sends.at[stage, unit_index],
                recv_sem=recvs.at[stage, unit_index],
                device_id=(gx, to_y),
                device_id_type=MESH,
            ).start()

    def scatter_fields(u):
        parts = granules(UNITS[u])
        for i in range(N_GY):
            for g in range(parts):
                start = UNITS[u][1] + (i * parts + g) * GRANULE
                fields[u][i, g] = acc[start : start + GRANULE].astype(jnp.bfloat16)
        to_peers(fields[u], gathered[u], lambda device: device, 0, u)

    def frequency_slot(device):
        freq = rem(device, 2) * 8 + rem(div(device, 2), 2) * 4
        freq = freq + rem(div(device, 4), 2) * 2 + div(device, 8)
        return 8 - (freq - 8) * (2 * div(freq, 8) - 1)

    def transform(u):
        pltpu.make_async_copy(gathered[u], gathered[u], recvs.at[0, u]).wait()
        for g in range(granules(UNITS[u])):
            for half in range(LANES // 128):
                lanes = slice(128 * half, 128 * half + 128)
                values = [gathered[u][s, g, :, lanes].astype(jnp.float32) for s in range(N_GY)]
                for r, (re, im) in enumerate(real_transform(values)):
                    im = jnp.zeros_like(re) if im is None else im
                    partials[u][r, g, 0, :, lanes] = re.astype(jnp.bfloat16)
                    partials[u][r, g, 1, :, lanes] = im.astype(jnp.bfloat16)
        to_peers(partials[u], outs[u], frequency_slot, 1, u)

    def run(pair, low, rows, first, last, phases, arriving=False, between=None):
        def step(i, carry):
            if between is not None:

                @pl.when(i == between[0])
                def _():
                    transform(between[1])

            for phase in range(phases if arriving else 0):
                arrived = recv.at[pl.ds(0, N_GY)]
                sem = route_recv.at[i * phases + phase]
                pltpu.make_async_copy(arrived, arrived, sem).wait()
            deposit(pair, low, rows, i * phases, phases)
            return carry

        lax.fori_loop(first // phases, last // phases, step, 0)

    acc[...] = jnp.zeros_like(acc)
    run(0, 0, ROWS, 0, 4, 1, arriving=True)
    run(0, 0, HALF, 4, N_GX, 2, arriving=True)
    scatter_fields(0)
    run(0, HALF, HALF, 4, N_GX, 2)
    scatter_fields(1)
    for u in range(2, count):
        if u % 2 == 0:
            acc[...] = jnp.zeros_like(acc)
        run(*UNITS[u], 0, N_GX, 4, between=(1, 0) if u == 2 else None)
        scatter_fields(u)
        transform(u - 1)

    def finish(u):
        pltpu.make_async_copy(outs[u], outs[u], recvs.at[1, u]).wait()
        pair, low, rows = UNITS[u]
        unit_lines(UNITS[u], matrix, outs[u], staged, 2 * pair, low // CY)
        for half in range(2):
            at = (half, pl.ds(2 * pair, 2), pl.ds(low // CY, rows // CY))
            copy = pltpu.make_async_copy(staged.at[at], done_ref.at[at], done_sems.at[u, half])
            copy.start()
            moved.append(copy)

    moved = [matrix_load]
    own_load.wait()
    for u in range(count - 2):
        finish(u)
    transform(count - 1)
    finish(count - 2)
    for copy in moved:
        copy.wait()

    sent = send_ref.at[pl.ds(0, DEVICES - 1)]
    pltpu.make_async_copy(sent, sent, route_send).wait()
    for u in range(count):
        sent = fields[u].at[pl.ds(0, N_GY - 1)]
        pltpu.make_async_copy(sent, sent, sends.at[0, u]).wait()
        sent = outs[u].at[pl.ds(0, N_GY - 1)]
        pltpu.make_async_copy(sent, sent, sends.at[1, u]).wait()
    pltpu.make_async_copy(outs[-1], outs[-1], recvs.at[1, count - 1]).wait()


def lines_kernel(matrix, part, done_ref, out_ref, last, sems):
    pair, low, rows = UNITS[-1]
    copies = []
    for half in range(2):
        for u in range(len(UNITS) - 1):
            at = (half, pl.ds(2 * UNITS[u][0], 2), pl.ds(UNITS[u][1] // CY, UNITS[u][2] // CY))
            copies.append((done_ref.at[at], out_ref.at[at]))
    for i, (source, target) in enumerate(copies):
        pltpu.make_async_copy(source, target, sems.at[i]).start()
    unit_lines(UNITS[-1], matrix, part, last, 0, 0)
    for half in range(2):
        at = (half, pl.ds(2 * pair, 2), pl.ds(low // CY, rows // CY))
        copies.append((last.at[half], out_ref.at[at]))
        i = len(copies) - 1
        pltpu.make_async_copy(*copies[i], sems.at[i]).start()
    for i, (source, target) in enumerate(copies):
        pltpu.make_async_copy(source, target, sems.at[i]).wait()


def line_table():
    y = np.arange(CY)
    q = np.arange(CY)
    tables = []
    for freq in range(N_GY):
        phase = (q[:, None] * N_GY + freq) * y[None, :] % (CY * N_GY)
        angle = phase * (2.0 * np.pi / (CY * N_GY))
        cos, sin = np.cos(angle), np.sin(angle)
        sign = -1.0 if freq > N_GY // 2 else 1.0
        full = np.stack([np.stack([cos, sign * sin], 1), np.stack([-sin, sign * cos], 1)])
        full = full.reshape(2, CY, 2, CY // GRANULE, GRANULE).transpose(0, 1, 3, 2, 4)
        full = full.reshape(2 * CY, 2 * CY)
        high = full.astype(jnp.bfloat16)
        tables.append(np.stack([high, (full - high.astype(np.float64)).astype(jnp.bfloat16)]))
    return np.stack(tables)


def shards(table, offsets, weights, owners, cells):
    unit_shapes = [(N_GY, granules(unit), GRANULE, LANES) for unit in UNITS]
    half_shapes = [(9, granules(unit), 2, GRANULE, LANES) for unit in UNITS]
    out_shapes = [(N_GY, granules(unit), 2, GRANULE, LANES) for unit in UNITS]
    part, matrix, done = pl.pallas_call(
        exchange_kernel,
        out_shape=[
            jax.ShapeDtypeStruct(out_shapes[-1], jnp.bfloat16),
            jax.ShapeDtypeStruct((2, 2 * CY, 2 * CY), jnp.bfloat16),
            jax.ShapeDtypeStruct((2, 6, CX, CY, NZ), jnp.float32),
        ],
        in_specs=[HBM] * 5,
        out_specs=[ANY] * 3,
        scratch_shapes=[
            *[pltpu.VMEM(shape, jnp.bfloat16) for shape in out_shapes[:-1]],
            *[pltpu.VMEM(shape, jnp.bfloat16) for shape in unit_shapes],
            *[pltpu.VMEM(shape, jnp.bfloat16) for shape in unit_shapes],
            *[pltpu.VMEM(shape, jnp.bfloat16) for shape in half_shapes],
            pltpu.VMEM((1, NB), jnp.int32),
            pltpu.VMEM((NB, 3, BP), jnp.float32),
            pltpu.VMEM((NB, BP), jnp.float32),
            pltpu.VMEM((NB, BP), jnp.int32),
            pltpu.VMEM((DEVICES * CAP * 8, BP), jnp.float32),
            pltpu.VMEM((DEVICES, CAP, 8, BP), jnp.bfloat16),
            pltpu.VMEM((DEVICES, CAP, 8, BP), jnp.bfloat16),
            pltpu.VMEM((ROWS, LANES), jnp.float32),
            pltpu.VMEM((2, 2 * CY, 2 * CY), jnp.bfloat16),
            pltpu.VMEM((2, 6, CX, CY, NZ), jnp.float32),
            pltpu.SemaphoreType.DMA((6,)),
            pltpu.SemaphoreType.DMA,
            pltpu.SemaphoreType.DMA((N_GX,)),
            pltpu.SemaphoreType.DMA((2, len(UNITS))),
            pltpu.SemaphoreType.DMA((2, len(UNITS))),
            pltpu.SemaphoreType.DMA((len(UNITS) - 1, 2)),
        ],
        compiler_params=pltpu.CompilerParams(
            has_side_effects=True, collective_id=0, vmem_limit_bytes=48 << 20
        ),
        name="exchange",
    )(
        *[
            pltpu.with_memory_space_constraint(array, pltpu.HBM)
            for array in (
                owners.reshape(1, NB),
                jnp.transpose(offsets.reshape(3, NB, BP), (1, 0, 2)),
                weights.reshape(NB, BP),
                cells.reshape(NB, BP),
                table,
            )
        ]
    )
    return pl.pallas_call(
        lines_kernel,
        out_shape=jax.ShapeDtypeStruct((2, 6, CX, CY, NZ), jnp.float32),
        in_specs=[VMEM] * 3,
        out_specs=HBM,
        scratch_shapes=[
            pltpu.VMEM((2, 2, UNITS[-1][2] // CY, CY, NZ), jnp.float32),
            pltpu.SemaphoreType.DMA((2 * len(UNITS),)),
        ],
        compiler_params=pltpu.CompilerParams(vmem_limit_bytes=8 << 20),
        name="lines",
    )(matrix, part, done)


def solution(mesh):
    table = line_table()
    placed = (P(None, ("gx", "gy")), P(("gx", "gy")), P(("gx", "gy"), None), P(("gx", "gy")))
    mapped = jax.shard_map(
        shards,
        mesh=mesh,
        in_specs=(P(),) + placed,
        out_specs=P(None, None, "gx", "gy", None),
        check_vma=False,
    )
    return functools.partial(mapped, jnp.asarray(table))
```

```python
import functools
import math

import jax
import jax.numpy as jnp
import numpy as np
from jax import lax
from jax.experimental import pallas as pl
from jax.experimental.pallas import tpu as pltpu
from jax.sharding import PartitionSpec as P

CX = 8
CY = 64
NZ = 128
BP = 128
CAP = 2
NB = 128
N_GX = 8
N_GY = 16
DEVICES = N_GX * N_GY
ROWS = CX * CY
LANES = 2 * NZ
GRANULE = 16
HALF = ROWS // 2
UNITS = tuple((pair, low, HALF) for pair in range(3) for low in (0, HALF))
MESH = pl.DeviceIdType.MESH
ANY = pl.BlockSpec(memory_space=pl.ANY)
HBM = pl.BlockSpec(memory_space=pltpu.HBM)
VMEM = pl.BlockSpec(memory_space=pltpu.VMEM)


def granules(unit):
    return unit[2] // (N_GY * GRANULE)


def hops(offset):
    return sum(min(step, 4 - step) for step in offset)


def offsets_by_distance(with_z):
    span = range(4) if with_z else range(1)
    cores = range(2) if with_z else range(1)
    every = [(z, c, y, x) for z in span for c in cores for y in range(4) for x in range(4)]
    return sorted(every, key=lambda o: (hops((o[0], o[2], o[3])), o[1]))


ROUTE = offsets_by_distance(True)
PLANE = offsets_by_distance(False)


def reversed4(value):
    return value % 2 * 8 + value // 2 % 2 * 4 + value // 4 % 2 * 2 + value // 8


def real_transform(values):
    count = len(values)
    if count == 2:
        return [(values[0] + values[1], None), (values[0] - values[1], None)]
    even = real_transform(values[::2])
    odd = real_transform(values[1::2])
    half = count // 2

    def at(spectrum, k):
        if k <= half // 2:
            return spectrum[k]
        re, im = spectrum[half - k]
        return re, None if im is None else -im

    result = []
    for k in range(half + 1):
        ere, eim = at(even, k % half)
        ore, oim = at(odd, k % half)
        if k == 0 or k == half:
            pre, pim = (ore, oim) if k == 0 else (-ore, None if oim is None else -oim)
        elif 4 * k == count:
            pre, pim = (oim, -ore)
        else:
            angle = 2.0 * math.pi * k / count
            cos, sin = math.cos(angle), math.sin(angle)
            if oim is None:
                pre, pim = ore * cos, ore * -sin
            else:
                pre, pim = ore * cos + oim * sin, oim * cos - ore * sin

        def plus(u, v):
            return v if u is None else u if v is None else u + v

        result.append((plus(ere, pre), plus(eim, pim)))
    return result


def write_slots(owner, offsets, weights, cells, planes, send_ref):
    a, b, c = (offsets[:, i, :] for i in range(3))
    scaled = weights / jnp.maximum(a * a + b * b + c * c, 0.25)
    pairs = ((a, a), (b, b), (c, c), (a, b), (b, c), (c, a))
    values = [(first * second * scaled).astype(jnp.bfloat16) for first, second in pairs]
    row = (cells >> 7) - ROWS // 2
    values += [code.astype(jnp.float32).astype(jnp.bfloat16) for code in (row, cells & (NZ - 1))]
    across = jnp.broadcast_to(owner.astype(jnp.float32), (NB, NB))
    same = jnp.where(across == across.T, 1.0, 0.0)
    block = lax.broadcasted_iota(jnp.int32, (NB, NB), 0)
    before = jnp.where(block < lax.broadcasted_iota(jnp.int32, (NB, NB), 1), same, 0.0)
    slot = owner.astype(jnp.float32) * CAP + jnp.sum(before, axis=0, keepdims=True)
    slots = lax.broadcasted_iota(jnp.int32, (DEVICES * CAP, NB), 0).astype(jnp.float32)
    hot = jnp.where(slots == slot, 1.0, 0.0).astype(jnp.bfloat16)
    for k, value in enumerate(values):
        placed = jnp.dot(hot, value, preferred_element_type=jnp.float32)
        planes[pl.ds(k, DEVICES * CAP, stride=8), :] = placed
    send_ref[...] = planes[...].reshape(DEVICES, CAP, 8, BP).astype(jnp.bfloat16)


def unit_lines(unit, matrix, part, target, first_k, first_x):
    sources = N_GY * CY // unit[2]
    for x in range(unit[2] // CY):
        values = part[sources * x : sources * x + sources].reshape(2 * CY, LANES)
        lines = jnp.dot(matrix[0], values, preferred_element_type=jnp.float32)
        lines += jnp.dot(matrix[1], values, preferred_element_type=jnp.float32)
        for half in range(2):
            for k in range(2):
                target[half, first_k + k, first_x + x] = lines[
                    half * CY : half * CY + CY, k * NZ : k * NZ + NZ
                ]


def exchange_kernel(owner_hbm, offset_hbm, weight_hbm, cell_hbm, table_hbm, *refs):
    count = len(UNITS)
    (last_ref, matrix_ref, done_ref), refs = refs[:3], refs[3:]
    outs, refs = (*refs[: count - 1], last_ref), refs[count - 1 :]
    fields, refs = refs[:count], refs[count:]
    gathered, refs = refs[:count], refs[count:]
    partials, refs = refs[:count], refs[count:]
    owner_ref, offset_ref, weight_ref, cell_ref, planes, send_ref, recv, acc = refs[:8]
    matrix, staged, load_sems, route_send, route_recv, sends, recvs, done_sems = refs[8:]
    gx = lax.axis_index("gx")
    gy = lax.axis_index("gy")
    me = gx * N_GY + gy

    loads = [
        pltpu.make_async_copy(source, target, load_sems.at[i])
        for i, (source, target) in enumerate(
            (
                (owner_hbm, owner_ref),
                (offset_hbm, offset_ref),
                (weight_hbm, weight_ref),
                (cell_hbm, cell_ref),
            )
        )
    ]
    barrier = pltpu.get_barrier_semaphore()

    rem, div = lax.rem, lax.div
    columns = {
        (z, c): rem(div(gx, 2) + z, 4) * 2 + rem(gx + c, 2) for z in range(4) for c in range(2)
    }
    places = {
        (y, x): rem(div(gy, 4) + y, 4) * 4 + rem(gy + x, 4) for y in range(4) for x in range(4)
    }
    routes = [(columns[offset[:2]], places[offset[2:]]) for offset in ROUTE]
    peers = [places[offset[2:]] for offset in PLANE[1:]]
    for device in routes[:0:-1]:
        pl.semaphore_signal(barrier, inc=1, device_id=device, device_id_type=MESH)
    for load in loads:
        load.start()
    matrix_load = pltpu.make_async_copy(
        table_hbm.at[reversed4(gy)], matrix_ref, load_sems.at[len(loads)]
    )
    matrix_load.start()
    own_load = pltpu.make_async_copy(table_hbm.at[reversed4(gy)], matrix, load_sems.at[5])
    own_load.start()
    for load in loads:
        load.wait()
    write_slots(owner_ref[...], offset_ref, weight_ref[...], cell_ref[...], planes, send_ref)
    pl.semaphore_wait(barrier, DEVICES - 1)

    pltpu.make_async_copy(send_ref.at[me], recv.at[0], route_recv.at[0]).start()
    for i, device in enumerate(routes):
        if i:
            pltpu.make_async_remote_copy(
                src_ref=send_ref.at[device[0] * N_GY + device[1]],
                dst_ref=recv.at[i],
                send_sem=route_send,
                recv_sem=route_recv.at[i // N_GY],
                device_id=device,
                device_id_type=MESH,
            ).start()

    depth_index = lax.broadcasted_iota(jnp.int32, (NZ, BP), 0)
    depth_index = depth_index.astype(jnp.float32).astype(jnp.bfloat16)
    one_value = jnp.ones((), jnp.bfloat16)
    zero_value = jnp.zeros((), jnp.bfloat16)

    def deposit(pair, low, rows, first, phases):
        row_index = lax.broadcasted_iota(jnp.int32, (rows, BP), 0) + (low - ROWS // 2)
        row_index = row_index.astype(jnp.float32).astype(jnp.bfloat16)
        row_hot, spread = [], []
        for phase in range(phases):
            base = (first + phase) * N_GY
            for slot in range(N_GY * CAP):
                block = recv[base + slot // CAP, slot % CAP]
                row = jnp.broadcast_to(block[6:7], (rows, BP))
                depth = jnp.broadcast_to(block[7:8], (NZ, BP)) == depth_index
                row_hot.append(jnp.where(row == row_index, one_value, zero_value))
                terms = [
                    jnp.where(depth, jnp.broadcast_to(block[k : k + 1], (NZ, BP)), zero_value)
                    for k in (2 * pair, 2 * pair + 1)
                ]
                spread.append(jnp.concatenate(terms, axis=0))
        acc[low : low + rows] += lax.dot_general(
            jnp.concatenate(row_hot, axis=1),
            jnp.concatenate(spread, axis=1),
            (((1,), (1,)), ((), ())),
            preferred_element_type=jnp.float32,
        )

    def to_peers(sources, target, slot_of, stage, unit_index):
        pltpu.make_async_copy(
            sources.at[slot_of(gy)], target.at[gy], recvs.at[stage, unit_index]
        ).start()

        for to_y in peers:
            pltpu.make_async_remote_copy(
                src_ref=sources.at[slot_of(to_y)],
                dst_ref=target.at[gy],
                send_sem=sends.at[stage, unit_index],
                recv_sem=recvs.at[stage, unit_index],
                device_id=(gx, to_y),
                device_id_type=MESH,
            ).start()

    def scatter_fields(u):
        parts = granules(UNITS[u])
        for i in range(N_GY):
            for g in range(parts):
                start = UNITS[u][1] + (i * parts + g) * GRANULE
                fields[u][i, g] = acc[start : start + GRANULE].astype(jnp.bfloat16)
        to_peers(fields[u], gathered[u], lambda device: device, 0, u)

    def frequency_slot(device):
        freq = rem(device, 2) * 8 + rem(div(device, 2), 2) * 4
        freq = freq + rem(div(device, 4), 2) * 2 + div(device, 8)
        return 8 - (freq - 8) * (2 * div(freq, 8) - 1)

    def transform(u):
        pltpu.make_async_copy(gathered[u], gathered[u], recvs.at[0, u]).wait()
        for g in range(granules(UNITS[u])):
            for half in range(LANES // 128):
                lanes = slice(128 * half, 128 * half + 128)
                values = [gathered[u][s, g, :, lanes].astype(jnp.float32) for s in range(N_GY)]
                for r, (re, im) in enumerate(real_transform(values)):
                    im = jnp.zeros_like(re) if im is None else im
                    partials[u][r, g, 0, :, lanes] = re.astype(jnp.bfloat16)
                    partials[u][r, g, 1, :, lanes] = im.astype(jnp.bfloat16)
        to_peers(partials[u], outs[u], frequency_slot, 1, u)

    def run(pair, low, rows, first, last, phases, arriving=False, between=None):
        def step(i, carry):
            if between is not None:

                @pl.when(i == between[0])
                def _():
                    transform(between[1])

            for phase in range(phases if arriving else 0):
                arrived = recv.at[pl.ds(0, N_GY)]
                sem = route_recv.at[i * phases + phase]
                pltpu.make_async_copy(arrived, arrived, sem).wait()
            deposit(pair, low, rows, i * phases, phases)
            return carry

        lax.fori_loop(first // phases, last // phases, step, 0)

    acc[...] = jnp.zeros_like(acc)
    run(0, 0, ROWS, 0, 4, 1, arriving=True)
    run(0, 0, HALF, 4, N_GX, 1, arriving=True)
    scatter_fields(0)
    run(0, HALF, HALF, 4, N_GX, 2)
    scatter_fields(1)
    for u in range(2, count):
        if u % 2 == 0:
            acc[...] = jnp.zeros_like(acc)
        run(*UNITS[u], 0, N_GX, 4, between=(1, 0) if u == 2 else None)
        scatter_fields(u)
        transform(u - 1)

    def finish(u):
        pltpu.make_async_copy(outs[u], outs[u], recvs.at[1, u]).wait()
        pair, low, rows = UNITS[u]
        unit_lines(UNITS[u], matrix, outs[u], staged, 2 * pair, low // CY)
        for half in range(2):
            at = (half, pl.ds(2 * pair, 2), pl.ds(low // CY, rows // CY))
            copy = pltpu.make_async_copy(staged.at[at], done_ref.at[at], done_sems.at[u, half])
            copy.start()
            moved.append(copy)

    moved = [matrix_load]
    own_load.wait()
    for u in range(count - 3):
        finish(u)
    transform(count - 1)
    finish(count - 3)
    finish(count - 2)
    for copy in moved:
        copy.wait()

    sent = send_ref.at[pl.ds(0, DEVICES - 1)]
    pltpu.make_async_copy(sent, sent, route_send).wait()
    for u in range(count):
        sent = fields[u].at[pl.ds(0, N_GY - 1)]
        pltpu.make_async_copy(sent, sent, sends.at[0, u]).wait()
        sent = outs[u].at[pl.ds(0, N_GY - 1)]
        pltpu.make_async_copy(sent, sent, sends.at[1, u]).wait()
    pltpu.make_async_copy(outs[-1], outs[-1], recvs.at[1, count - 1]).wait()


def lines_kernel(matrix, part, done_ref, out_ref, last, sems):
    pair, low, rows = UNITS[-1]
    copies = []
    for half in range(2):
        for u in range(len(UNITS) - 1):
            at = (half, pl.ds(2 * UNITS[u][0], 2), pl.ds(UNITS[u][1] // CY, UNITS[u][2] // CY))
            copies.append((done_ref.at[at], out_ref.at[at]))
    for i, (source, target) in enumerate(copies):
        pltpu.make_async_copy(source, target, sems.at[i]).start()
    unit_lines(UNITS[-1], matrix, part, last, 0, 0)
    for half in range(2):
        at = (half, pl.ds(2 * pair, 2), pl.ds(low // CY, rows // CY))
        copies.append((last.at[half], out_ref.at[at]))
        i = len(copies) - 1
        pltpu.make_async_copy(*copies[i], sems.at[i]).start()
    for i, (source, target) in enumerate(copies):
        pltpu.make_async_copy(source, target, sems.at[i]).wait()


def line_table():
    y = np.arange(CY)
    q = np.arange(CY)
    tables = []
    for freq in range(N_GY):
        phase = (q[:, None] * N_GY + freq) * y[None, :] % (CY * N_GY)
        angle = phase * (2.0 * np.pi / (CY * N_GY))
        cos, sin = np.cos(angle), np.sin(angle)
        sign = -1.0 if freq > N_GY // 2 else 1.0
        full = np.stack([np.stack([cos, sign * sin], 1), np.stack([-sin, sign * cos], 1)])
        full = full.reshape(2, CY, 2, CY // GRANULE, GRANULE).transpose(0, 1, 3, 2, 4)
        full = full.reshape(2 * CY, 2 * CY)
        high = full.astype(jnp.bfloat16)
        tables.append(np.stack([high, (full - high.astype(np.float64)).astype(jnp.bfloat16)]))
    return np.stack(tables)


def shards(table, offsets, weights, owners, cells):
    unit_shapes = [(N_GY, granules(unit), GRANULE, LANES) for unit in UNITS]
    half_shapes = [(9, granules(unit), 2, GRANULE, LANES) for unit in UNITS]
    out_shapes = [(N_GY, granules(unit), 2, GRANULE, LANES) for unit in UNITS]
    part, matrix, done = pl.pallas_call(
        exchange_kernel,
        out_shape=[
            jax.ShapeDtypeStruct(out_shapes[-1], jnp.bfloat16),
            jax.ShapeDtypeStruct((2, 2 * CY, 2 * CY), jnp.bfloat16),
            jax.ShapeDtypeStruct((2, 6, CX, CY, NZ), jnp.float32),
        ],
        in_specs=[HBM] * 5,
        out_specs=[ANY] * 3,
        scratch_shapes=[
            *[pltpu.VMEM(shape, jnp.bfloat16) for shape in out_shapes[:-1]],
            *[pltpu.VMEM(shape, jnp.bfloat16) for shape in unit_shapes],
            *[pltpu.VMEM(shape, jnp.bfloat16) for shape in unit_shapes],
            *[pltpu.VMEM(shape, jnp.bfloat16) for shape in half_shapes],
            pltpu.VMEM((1, NB), jnp.int32),
            pltpu.VMEM((NB, 3, BP), jnp.float32),
            pltpu.VMEM((NB, BP), jnp.float32),
            pltpu.VMEM((NB, BP), jnp.int32),
            pltpu.VMEM((DEVICES * CAP * 8, BP), jnp.float32),
            pltpu.VMEM((DEVICES, CAP, 8, BP), jnp.bfloat16),
            pltpu.VMEM((DEVICES, CAP, 8, BP), jnp.bfloat16),
            pltpu.VMEM((ROWS, LANES), jnp.float32),
            pltpu.VMEM((2, 2 * CY, 2 * CY), jnp.bfloat16),
            pltpu.VMEM((2, 6, CX, CY, NZ), jnp.float32),
            pltpu.SemaphoreType.DMA((6,)),
            pltpu.SemaphoreType.DMA,
            pltpu.SemaphoreType.DMA((N_GX,)),
            pltpu.SemaphoreType.DMA((2, len(UNITS))),
            pltpu.SemaphoreType.DMA((2, len(UNITS))),
            pltpu.SemaphoreType.DMA((len(UNITS) - 1, 2)),
        ],
        compiler_params=pltpu.CompilerParams(
            has_side_effects=True, collective_id=0, vmem_limit_bytes=48 << 20
        ),
        name="exchange",
    )(
        *[
            pltpu.with_memory_space_constraint(array, pltpu.HBM)
            for array in (
                owners.reshape(1, NB),
                jnp.transpose(offsets.reshape(3, NB, BP), (1, 0, 2)),
                weights.reshape(NB, BP),
                cells.reshape(NB, BP),
                table,
            )
        ]
    )
    return pl.pallas_call(
        lines_kernel,
        out_shape=jax.ShapeDtypeStruct((2, 6, CX, CY, NZ), jnp.float32),
        in_specs=[VMEM] * 3,
        out_specs=HBM,
        scratch_shapes=[
            pltpu.VMEM((2, 2, UNITS[-1][2] // CY, CY, NZ), jnp.float32),
            pltpu.SemaphoreType.DMA((2 * len(UNITS),)),
        ],
        compiler_params=pltpu.CompilerParams(vmem_limit_bytes=8 << 20),
        name="lines",
    )(matrix, part, done)


def solution(mesh):
    table = line_table()
    placed = (P(None, ("gx", "gy")), P(("gx", "gy")), P(("gx", "gy"), None), P(("gx", "gy")))
    mapped = jax.shard_map(
        shards,
        mesh=mesh,
        in_specs=(P(),) + placed,
        out_specs=P(None, None, "gx", "gy", None),
        check_vma=False,
    )
    return functools.partial(mapped, jnp.asarray(table))
```

```python
import functools
import math

import jax
import jax.numpy as jnp
import numpy as np
from jax import lax
from jax.experimental import pallas as pl
from jax.experimental.pallas import tpu as pltpu
from jax.sharding import PartitionSpec as P

CX = 8
CY = 64
NZ = 128
BP = 128
CAP = 2
NB = 128
N_GX = 8
N_GY = 16
DEVICES = N_GX * N_GY
ROWS = CX * CY
LANES = 2 * NZ
GRANULE = 16
HALF = ROWS // 2
UNITS = tuple((pair, low, HALF) for pair in range(3) for low in (0, HALF))
MESH = pl.DeviceIdType.MESH
ANY = pl.BlockSpec(memory_space=pl.ANY)
HBM = pl.BlockSpec(memory_space=pltpu.HBM)
VMEM = pl.BlockSpec(memory_space=pltpu.VMEM)


def granules(unit):
    return unit[2] // (N_GY * GRANULE)


def hops(offset):
    return sum(min(step, 4 - step) for step in offset)


def offsets_by_distance(with_z):
    span = range(4) if with_z else range(1)
    cores = range(2) if with_z else range(1)
    every = [(z, c, y, x) for z in span for c in cores for y in range(4) for x in range(4)]
    return sorted(every, key=lambda o: (hops((o[0], o[2], o[3])), o[1]))


ROUTE = offsets_by_distance(True)
PLANE = offsets_by_distance(False)


def reversed4(value):
    return value % 2 * 8 + value // 2 % 2 * 4 + value // 4 % 2 * 2 + value // 8


def real_transform(values):
    count = len(values)
    if count == 2:
        return [(values[0] + values[1], None), (values[0] - values[1], None)]
    even = real_transform(values[::2])
    odd = real_transform(values[1::2])
    half = count // 2

    def at(spectrum, k):
        if k <= half // 2:
            return spectrum[k]
        re, im = spectrum[half - k]
        return re, None if im is None else -im

    result = []
    for k in range(half + 1):
        ere, eim = at(even, k % half)
        ore, oim = at(odd, k % half)
        if k == 0 or k == half:
            pre, pim = (ore, oim) if k == 0 else (-ore, None if oim is None else -oim)
        elif 4 * k == count:
            pre, pim = (oim, -ore)
        else:
            angle = 2.0 * math.pi * k / count
            cos, sin = math.cos(angle), math.sin(angle)
            if oim is None:
                pre, pim = ore * cos, ore * -sin
            else:
                pre, pim = ore * cos + oim * sin, oim * cos - ore * sin

        def plus(u, v):
            return v if u is None else u if v is None else u + v

        result.append((plus(ere, pre), plus(eim, pim)))
    return result


def write_slots(owner, offsets, weights, cells, planes, send_ref):
    a, b, c = (offsets[:, i, :] for i in range(3))
    scaled = weights / jnp.maximum(a * a + b * b + c * c, 0.25)
    pairs = ((a, a), (b, b), (c, c), (a, b), (b, c), (c, a))
    values = [(first * second * scaled).astype(jnp.bfloat16) for first, second in pairs]
    row = (cells >> 7) - ROWS // 2
    values += [code.astype(jnp.float32).astype(jnp.bfloat16) for code in (row, cells & (NZ - 1))]
    across = jnp.broadcast_to(owner.astype(jnp.float32), (NB, NB))
    same = jnp.where(across == across.T, 1.0, 0.0)
    block = lax.broadcasted_iota(jnp.int32, (NB, NB), 0)
    before = jnp.where(block < lax.broadcasted_iota(jnp.int32, (NB, NB), 1), same, 0.0)
    slot = owner.astype(jnp.float32) * CAP + jnp.sum(before, axis=0, keepdims=True)
    slots = lax.broadcasted_iota(jnp.int32, (DEVICES * CAP, NB), 0).astype(jnp.float32)
    hot = jnp.where(slots == slot, 1.0, 0.0).astype(jnp.bfloat16)
    for k, value in enumerate(values):
        placed = jnp.dot(hot, value, preferred_element_type=jnp.float32)
        planes[pl.ds(k, DEVICES * CAP, stride=8), :] = placed
    send_ref[...] = planes[...].reshape(DEVICES, CAP, 8, BP).astype(jnp.bfloat16)


def unit_lines(unit, matrix, part, target, first_k, first_x):
    sources = N_GY * CY // unit[2]
    for x in range(unit[2] // CY):
        values = part[sources * x : sources * x + sources].reshape(2 * CY, LANES)
        lines = jnp.dot(matrix[0], values, preferred_element_type=jnp.float32)
        lines += jnp.dot(matrix[1], values, preferred_element_type=jnp.float32)
        for half in range(2):
            for k in range(2):
                target[half, first_k + k, first_x + x] = lines[
                    half * CY : half * CY + CY, k * NZ : k * NZ + NZ
                ]


def exchange_kernel(owner_hbm, offset_hbm, weight_hbm, cell_hbm, table_hbm, *refs):
    count = len(UNITS)
    (last_ref, matrix_ref, done_ref), refs = refs[:3], refs[3:]
    outs, refs = (*refs[: count - 1], last_ref), refs[count - 1 :]
    fields, refs = refs[:count], refs[count:]
    gathered, refs = refs[:count], refs[count:]
    partials, refs = refs[:count], refs[count:]
    owner_ref, offset_ref, weight_ref, cell_ref, planes, send_ref, recv, acc = refs[:8]
    matrix, staged, load_sems, route_send, route_recv, sends, recvs, done_sems = refs[8:]
    gx = lax.axis_index("gx")
    gy = lax.axis_index("gy")
    me = gx * N_GY + gy

    loads = [
        pltpu.make_async_copy(source, target, load_sems.at[i])
        for i, (source, target) in enumerate(
            (
                (owner_hbm, owner_ref),
                (offset_hbm, offset_ref),
                (weight_hbm, weight_ref),
                (cell_hbm, cell_ref),
            )
        )
    ]
    barrier = pltpu.get_barrier_semaphore()

    rem, div = lax.rem, lax.div
    columns = {
        (z, c): rem(div(gx, 2) + z, 4) * 2 + rem(gx + c, 2) for z in range(4) for c in range(2)
    }
    places = {
        (y, x): rem(div(gy, 4) + y, 4) * 4 + rem(gy + x, 4) for y in range(4) for x in range(4)
    }
    routes = [(columns[offset[:2]], places[offset[2:]]) for offset in ROUTE]
    peers = [places[offset[2:]] for offset in PLANE[1:]]
    for device in routes[:0:-1]:
        pl.semaphore_signal(barrier, inc=1, device_id=device, device_id_type=MESH)
    for load in loads:
        load.start()
    matrix_load = pltpu.make_async_copy(
        table_hbm.at[reversed4(gy)], matrix_ref, load_sems.at[len(loads)]
    )
    matrix_load.start()
    own_load = pltpu.make_async_copy(table_hbm.at[reversed4(gy)], matrix, load_sems.at[5])
    own_load.start()
    for load in loads:
        load.wait()
    write_slots(owner_ref[...], offset_ref, weight_ref[...], cell_ref[...], planes, send_ref)
    pl.semaphore_wait(barrier, DEVICES - 1)

    pltpu.make_async_copy(send_ref.at[me], recv.at[0], route_recv.at[0]).start()
    for i, device in enumerate(routes):
        if i:
            pltpu.make_async_remote_copy(
                src_ref=send_ref.at[device[0] * N_GY + device[1]],
                dst_ref=recv.at[i],
                send_sem=route_send,
                recv_sem=route_recv.at[i // N_GY],
                device_id=device,
                device_id_type=MESH,
            ).start()

    depth_index = lax.broadcasted_iota(jnp.int32, (NZ, BP), 0)
    depth_index = depth_index.astype(jnp.float32).astype(jnp.bfloat16)
    one_value = jnp.ones((), jnp.bfloat16)
    zero_value = jnp.zeros((), jnp.bfloat16)

    def deposit(pair, low, rows, first, phases):
        row_index = lax.broadcasted_iota(jnp.int32, (rows, BP), 0) + (low - ROWS // 2)
        row_index = row_index.astype(jnp.float32).astype(jnp.bfloat16)
        row_hot, spread = [], []
        for phase in range(phases):
            base = (first + phase) * N_GY
            for slot in range(N_GY * CAP):
                block = recv[base + slot // CAP, slot % CAP]
                row = jnp.broadcast_to(block[6:7], (rows, BP))
                depth = jnp.broadcast_to(block[7:8], (NZ, BP)) == depth_index
                row_hot.append(jnp.where(row == row_index, one_value, zero_value))
                terms = [
                    jnp.where(depth, jnp.broadcast_to(block[k : k + 1], (NZ, BP)), zero_value)
                    for k in (2 * pair, 2 * pair + 1)
                ]
                spread.append(jnp.concatenate(terms, axis=0))
        acc[low : low + rows] += lax.dot_general(
            jnp.concatenate(row_hot, axis=1),
            jnp.concatenate(spread, axis=1),
            (((1,), (1,)), ((), ())),
            preferred_element_type=jnp.float32,
        )

    def to_peers(sources, target, slot_of, stage, unit_index):
        pltpu.make_async_copy(
            sources.at[slot_of(gy)], target.at[gy], recvs.at[stage, unit_index]
        ).start()

        for to_y in peers:
            pltpu.make_async_remote_copy(
                src_ref=sources.at[slot_of(to_y)],
                dst_ref=target.at[gy],
                send_sem=sends.at[stage, unit_index],
                recv_sem=recvs.at[stage, unit_index],
                device_id=(gx, to_y),
                device_id_type=MESH,
            ).start()

    def scatter_fields(u):
        parts = granules(UNITS[u])
        for i in range(N_GY):
            for g in range(parts):
                start = UNITS[u][1] + (i * parts + g) * GRANULE
                fields[u][i, g] = acc[start : start + GRANULE].astype(jnp.bfloat16)
        to_peers(fields[u], gathered[u], lambda device: device, 0, u)

    def frequency_slot(device):
        freq = rem(device, 2) * 8 + rem(div(device, 2), 2) * 4
        freq = freq + rem(div(device, 4), 2) * 2 + div(device, 8)
        return 8 - (freq - 8) * (2 * div(freq, 8) - 1)

    def transform(u):
        pltpu.make_async_copy(gathered[u], gathered[u], recvs.at[0, u]).wait()
        for g in range(granules(UNITS[u])):
            for half in range(LANES // 128):
                lanes = slice(128 * half, 128 * half + 128)
                values = [gathered[u][s, g, :, lanes].astype(jnp.float32) for s in range(N_GY)]
                for r, (re, im) in enumerate(real_transform(values)):
                    im = jnp.zeros_like(re) if im is None else im
                    partials[u][r, g, 0, :, lanes] = re.astype(jnp.bfloat16)
                    partials[u][r, g, 1, :, lanes] = im.astype(jnp.bfloat16)
        to_peers(partials[u], outs[u], frequency_slot, 1, u)

    def run(pair, low, rows, first, last, phases, arriving=False, between=None):
        def step(i, carry):
            if between is not None:

                @pl.when(i == between[0])
                def _():
                    transform(between[1])

            for phase in range(phases if arriving else 0):
                arrived = recv.at[pl.ds(0, N_GY)]
                sem = route_recv.at[i * phases + phase]
                pltpu.make_async_copy(arrived, arrived, sem).wait()
            deposit(pair, low, rows, i * phases, phases)
            return carry

        lax.fori_loop(first // phases, last // phases, step, 0)

    acc[...] = jnp.zeros_like(acc)
    run(0, 0, ROWS, 0, 3, 1, arriving=True)
    run(0, 0, HALF, 3, N_GX, 1, arriving=True)
    scatter_fields(0)
    run(0, HALF, HALF, 3, N_GX, 1)
    scatter_fields(1)
    for u in range(2, count):
        if u % 2 == 0:
            acc[...] = jnp.zeros_like(acc)
        run(*UNITS[u], 0, N_GX, 4, between=(1, 0) if u == 2 else None)
        scatter_fields(u)
        transform(u - 1)

    def finish(u):
        pltpu.make_async_copy(outs[u], outs[u], recvs.at[1, u]).wait()
        pair, low, rows = UNITS[u]
        unit_lines(UNITS[u], matrix, outs[u], staged, 2 * pair, low // CY)
        for half in range(2):
            at = (half, pl.ds(2 * pair, 2), pl.ds(low // CY, rows // CY))
            copy = pltpu.make_async_copy(staged.at[at], done_ref.at[at], done_sems.at[u, half])
            copy.start()
            moved.append(copy)

    moved = [matrix_load]
    own_load.wait()
    for u in range(count - 3):
        finish(u)
    transform(count - 1)
    finish(count - 3)
    finish(count - 2)
    for copy in moved:
        copy.wait()

    sent = send_ref.at[pl.ds(0, DEVICES - 1)]
    pltpu.make_async_copy(sent, sent, route_send).wait()
    for u in range(count):
        sent = fields[u].at[pl.ds(0, N_GY - 1)]
        pltpu.make_async_copy(sent, sent, sends.at[0, u]).wait()
        sent = outs[u].at[pl.ds(0, N_GY - 1)]
        pltpu.make_async_copy(sent, sent, sends.at[1, u]).wait()
    pltpu.make_async_copy(outs[-1], outs[-1], recvs.at[1, count - 1]).wait()


def lines_kernel(matrix, part, done_ref, out_ref, last, sems):
    pair, low, rows = UNITS[-1]
    copies = []
    for half in range(2):
        for u in range(len(UNITS) - 1):
            at = (half, pl.ds(2 * UNITS[u][0], 2), pl.ds(UNITS[u][1] // CY, UNITS[u][2] // CY))
            copies.append((done_ref.at[at], out_ref.at[at]))
    for i, (source, target) in enumerate(copies):
        pltpu.make_async_copy(source, target, sems.at[i]).start()
    unit_lines(UNITS[-1], matrix, part, last, 0, 0)
    for half in range(2):
        at = (half, pl.ds(2 * pair, 2), pl.ds(low // CY, rows // CY))
        copies.append((last.at[half], out_ref.at[at]))
        i = len(copies) - 1
        pltpu.make_async_copy(*copies[i], sems.at[i]).start()
    for i, (source, target) in enumerate(copies):
        pltpu.make_async_copy(source, target, sems.at[i]).wait()


def line_table():
    y = np.arange(CY)
    q = np.arange(CY)
    tables = []
    for freq in range(N_GY):
        phase = (q[:, None] * N_GY + freq) * y[None, :] % (CY * N_GY)
        angle = phase * (2.0 * np.pi / (CY * N_GY))
        cos, sin = np.cos(angle), np.sin(angle)
        sign = -1.0 if freq > N_GY // 2 else 1.0
        full = np.stack([np.stack([cos, sign * sin], 1), np.stack([-sin, sign * cos], 1)])
        full = full.reshape(2, CY, 2, CY // GRANULE, GRANULE).transpose(0, 1, 3, 2, 4)
        full = full.reshape(2 * CY, 2 * CY)
        high = full.astype(jnp.bfloat16)
        tables.append(np.stack([high, (full - high.astype(np.float64)).astype(jnp.bfloat16)]))
    return np.stack(tables)


def shards(table, offsets, weights, owners, cells):
    unit_shapes = [(N_GY, granules(unit), GRANULE, LANES) for unit in UNITS]
    half_shapes = [(9, granules(unit), 2, GRANULE, LANES) for unit in UNITS]
    out_shapes = [(N_GY, granules(unit), 2, GRANULE, LANES) for unit in UNITS]
    part, matrix, done = pl.pallas_call(
        exchange_kernel,
        out_shape=[
            jax.ShapeDtypeStruct(out_shapes[-1], jnp.bfloat16),
            jax.ShapeDtypeStruct((2, 2 * CY, 2 * CY), jnp.bfloat16),
            jax.ShapeDtypeStruct((2, 6, CX, CY, NZ), jnp.float32),
        ],
        in_specs=[HBM] * 5,
        out_specs=[ANY] * 3,
        scratch_shapes=[
            *[pltpu.VMEM(shape, jnp.bfloat16) for shape in out_shapes[:-1]],
            *[pltpu.VMEM(shape, jnp.bfloat16) for shape in unit_shapes],
            *[pltpu.VMEM(shape, jnp.bfloat16) for shape in unit_shapes],
            *[pltpu.VMEM(shape, jnp.bfloat16) for shape in half_shapes],
            pltpu.VMEM((1, NB), jnp.int32),
            pltpu.VMEM((NB, 3, BP), jnp.float32),
            pltpu.VMEM((NB, BP), jnp.float32),
            pltpu.VMEM((NB, BP), jnp.int32),
            pltpu.VMEM((DEVICES * CAP * 8, BP), jnp.float32),
            pltpu.VMEM((DEVICES, CAP, 8, BP), jnp.bfloat16),
            pltpu.VMEM((DEVICES, CAP, 8, BP), jnp.bfloat16),
            pltpu.VMEM((ROWS, LANES), jnp.float32),
            pltpu.VMEM((2, 2 * CY, 2 * CY), jnp.bfloat16),
            pltpu.VMEM((2, 6, CX, CY, NZ), jnp.float32),
            pltpu.SemaphoreType.DMA((6,)),
            pltpu.SemaphoreType.DMA,
            pltpu.SemaphoreType.DMA((N_GX,)),
            pltpu.SemaphoreType.DMA((2, len(UNITS))),
            pltpu.SemaphoreType.DMA((2, len(UNITS))),
            pltpu.SemaphoreType.DMA((len(UNITS) - 1, 2)),
        ],
        compiler_params=pltpu.CompilerParams(
            has_side_effects=True, collective_id=0, vmem_limit_bytes=48 << 20
        ),
        name="exchange",
    )(
        *[
            pltpu.with_memory_space_constraint(array, pltpu.HBM)
            for array in (
                owners.reshape(1, NB),
                jnp.transpose(offsets.reshape(3, NB, BP), (1, 0, 2)),
                weights.reshape(NB, BP),
                cells.reshape(NB, BP),
                table,
            )
        ]
    )
    return pl.pallas_call(
        lines_kernel,
        out_shape=jax.ShapeDtypeStruct((2, 6, CX, CY, NZ), jnp.float32),
        in_specs=[VMEM] * 3,
        out_specs=HBM,
        scratch_shapes=[
            pltpu.VMEM((2, 2, UNITS[-1][2] // CY, CY, NZ), jnp.float32),
            pltpu.SemaphoreType.DMA((2 * len(UNITS),)),
        ],
        compiler_params=pltpu.CompilerParams(vmem_limit_bytes=8 << 20),
        name="lines",
    )(matrix, part, done)


def solution(mesh):
    table = line_table()
    placed = (P(None, ("gx", "gy")), P(("gx", "gy")), P(("gx", "gy"), None), P(("gx", "gy")))
    mapped = jax.shard_map(
        shards,
        mesh=mesh,
        in_specs=(P(),) + placed,
        out_specs=P(None, None, "gx", "gy", None),
        check_vma=False,
    )
    return functools.partial(mapped, jnp.asarray(table))
```

```python
import functools
import math

import jax
import jax.numpy as jnp
import numpy as np
from jax import lax
from jax.experimental import pallas as pl
from jax.experimental.pallas import tpu as pltpu
from jax.sharding import PartitionSpec as P

CX = 8
CY = 64
NZ = 128
BP = 128
CAP = 2
NB = 128
N_GX = 8
N_GY = 16
DEVICES = N_GX * N_GY
ROWS = CX * CY
LANES = 2 * NZ
GRANULE = 16
HALF = ROWS // 2
UNITS = tuple((pair, low, HALF) for pair in range(3) for low in (0, HALF))
MESH = pl.DeviceIdType.MESH
ANY = pl.BlockSpec(memory_space=pl.ANY)
HBM = pl.BlockSpec(memory_space=pltpu.HBM)
VMEM = pl.BlockSpec(memory_space=pltpu.VMEM)


def granules(unit):
    return unit[2] // (N_GY * GRANULE)


def hops(offset):
    return sum(min(step, 4 - step) for step in offset)


def offsets_by_distance(with_z):
    span = range(4) if with_z else range(1)
    cores = range(2) if with_z else range(1)
    every = [(z, c, y, x) for z in span for c in cores for y in range(4) for x in range(4)]
    return sorted(every, key=lambda o: (hops((o[0], o[2], o[3])), o[1]))


ROUTE = offsets_by_distance(True)
PLANE = offsets_by_distance(False)


def reversed4(value):
    return value % 2 * 8 + value // 2 % 2 * 4 + value // 4 % 2 * 2 + value // 8


def real_transform(values):
    count = len(values)
    if count == 2:
        return [(values[0] + values[1], None), (values[0] - values[1], None)]
    even = real_transform(values[::2])
    odd = real_transform(values[1::2])
    half = count // 2

    def at(spectrum, k):
        if k <= half // 2:
            return spectrum[k]
        re, im = spectrum[half - k]
        return re, None if im is None else -im

    result = []
    for k in range(half + 1):
        ere, eim = at(even, k % half)
        ore, oim = at(odd, k % half)
        if k == 0 or k == half:
            pre, pim = (ore, oim) if k == 0 else (-ore, None if oim is None else -oim)
        elif 4 * k == count:
            pre, pim = (oim, -ore)
        else:
            angle = 2.0 * math.pi * k / count
            cos, sin = math.cos(angle), math.sin(angle)
            if oim is None:
                pre, pim = ore * cos, ore * -sin
            else:
                pre, pim = ore * cos + oim * sin, oim * cos - ore * sin

        def plus(u, v):
            return v if u is None else u if v is None else u + v

        result.append((plus(ere, pre), plus(eim, pim)))
    return result


def write_slots(owner, offsets, weights, cells, planes, send_ref):
    a, b, c = (offsets[:, i, :] for i in range(3))
    scaled = weights / jnp.maximum(a * a + b * b + c * c, 0.25)
    pairs = ((a, a), (b, b), (c, c), (a, b), (b, c), (c, a))
    values = [(first * second * scaled).astype(jnp.bfloat16) for first, second in pairs]
    row = (cells >> 7) - ROWS // 2
    values += [code.astype(jnp.float32).astype(jnp.bfloat16) for code in (row, cells & (NZ - 1))]
    across = jnp.broadcast_to(owner.astype(jnp.float32), (NB, NB))
    same = jnp.where(across == across.T, 1.0, 0.0)
    block = lax.broadcasted_iota(jnp.int32, (NB, NB), 0)
    before = jnp.where(block < lax.broadcasted_iota(jnp.int32, (NB, NB), 1), same, 0.0)
    slot = owner.astype(jnp.float32) * CAP + jnp.sum(before, axis=0, keepdims=True)
    slots = lax.broadcasted_iota(jnp.int32, (DEVICES * CAP, NB), 0).astype(jnp.float32)
    hot = jnp.where(slots == slot, 1.0, 0.0).astype(jnp.bfloat16)
    for k, value in enumerate(values):
        placed = jnp.dot(hot, value, preferred_element_type=jnp.float32)
        planes[pl.ds(k, DEVICES * CAP, stride=8), :] = placed
    send_ref[...] = planes[...].reshape(DEVICES, CAP, 8, BP).astype(jnp.bfloat16)


def unit_lines(unit, matrix, part, target, first_k, first_x):
    sources = N_GY * CY // unit[2]
    for x in range(unit[2] // CY):
        values = part[sources * x : sources * x + sources].reshape(2 * CY, LANES)
        lines = jnp.dot(matrix[0], values, preferred_element_type=jnp.float32)
        lines += jnp.dot(matrix[1], values, preferred_element_type=jnp.float32)
        for half in range(2):
            for k in range(2):
                target[half, first_k + k, first_x + x] = lines[
                    half * CY : half * CY + CY, k * NZ : k * NZ + NZ
                ]


def exchange_kernel(owner_hbm, offset_hbm, weight_hbm, cell_hbm, table_hbm, *refs):
    count = len(UNITS)
    (last_ref, matrix_ref, done_ref), refs = refs[:3], refs[3:]
    outs, refs = (*refs[: count - 1], last_ref), refs[count - 1 :]
    fields, refs = refs[:count], refs[count:]
    gathered, refs = refs[:count], refs[count:]
    partials, refs = refs[:count], refs[count:]
    owner_ref, offset_ref, weight_ref, cell_ref, planes, send_ref, recv, acc = refs[:8]
    matrix, staged, load_sems, route_send, route_recv, sends, recvs, done_sems = refs[8:]
    gx = lax.axis_index("gx")
    gy = lax.axis_index("gy")
    me = gx * N_GY + gy

    loads = [
        pltpu.make_async_copy(source, target, load_sems.at[i])
        for i, (source, target) in enumerate(
            (
                (owner_hbm, owner_ref),
                (offset_hbm, offset_ref),
                (weight_hbm, weight_ref),
                (cell_hbm, cell_ref),
            )
        )
    ]
    barrier = pltpu.get_barrier_semaphore()

    rem, div = lax.rem, lax.div
    columns = {
        (z, c): rem(div(gx, 2) + z, 4) * 2 + rem(gx + c, 2) for z in range(4) for c in range(2)
    }
    places = {
        (y, x): rem(div(gy, 4) + y, 4) * 4 + rem(gy + x, 4) for y in range(4) for x in range(4)
    }
    routes = [(columns[offset[:2]], places[offset[2:]]) for offset in ROUTE]
    peers = [places[offset[2:]] for offset in PLANE[1:]]
    for device in routes[:0:-1]:
        pl.semaphore_signal(barrier, inc=1, device_id=device, device_id_type=MESH)
    for load in loads:
        load.start()
    matrix_load = pltpu.make_async_copy(
        table_hbm.at[reversed4(gy)], matrix_ref, load_sems.at[len(loads)]
    )
    matrix_load.start()
    own_load = pltpu.make_async_copy(table_hbm.at[reversed4(gy)], matrix, load_sems.at[5])
    own_load.start()
    for load in loads:
        load.wait()
    write_slots(owner_ref[...], offset_ref, weight_ref[...], cell_ref[...], planes, send_ref)
    pl.semaphore_wait(barrier, DEVICES - 1)

    pltpu.make_async_copy(send_ref.at[me], recv.at[0], route_recv.at[0]).start()
    for i, device in enumerate(routes):
        if i:
            pltpu.make_async_remote_copy(
                src_ref=send_ref.at[device[0] * N_GY + device[1]],
                dst_ref=recv.at[i],
                send_sem=route_send,
                recv_sem=route_recv.at[i // N_GY],
                device_id=device,
                device_id_type=MESH,
            ).start()

    depth_index = lax.broadcasted_iota(jnp.int32, (NZ, BP), 0)
    depth_index = depth_index.astype(jnp.float32).astype(jnp.bfloat16)
    one_value = jnp.ones((), jnp.bfloat16)
    zero_value = jnp.zeros((), jnp.bfloat16)

    def deposit(pair, low, rows, first, phases):
        row_index = lax.broadcasted_iota(jnp.int32, (rows, BP), 0) + (low - ROWS // 2)
        row_index = row_index.astype(jnp.float32).astype(jnp.bfloat16)
        row_hot, spread = [], []
        for phase in range(phases):
            base = (first + phase) * N_GY
            for slot in range(N_GY * CAP):
                block = recv[base + slot // CAP, slot % CAP]
                row = jnp.broadcast_to(block[6:7], (rows, BP))
                depth = jnp.broadcast_to(block[7:8], (NZ, BP)) == depth_index
                row_hot.append(jnp.where(row == row_index, one_value, zero_value))
                terms = [
                    jnp.where(depth, jnp.broadcast_to(block[k : k + 1], (NZ, BP)), zero_value)
                    for k in (2 * pair, 2 * pair + 1)
                ]
                spread.append(jnp.concatenate(terms, axis=0))
        acc[low : low + rows] += lax.dot_general(
            jnp.concatenate(row_hot, axis=1),
            jnp.concatenate(spread, axis=1),
            (((1,), (1,)), ((), ())),
            preferred_element_type=jnp.float32,
        )

    def to_peers(sources, target, slot_of, stage, unit_index):
        pltpu.make_async_copy(
            sources.at[slot_of(gy)], target.at[gy], recvs.at[stage, unit_index]
        ).start()

        ending = stage == 1 and unit_index == count - 1
        for to_y in peers[::-1] if ending else peers:
            pltpu.make_async_remote_copy(
                src_ref=sources.at[slot_of(to_y)],
                dst_ref=target.at[gy],
                send_sem=sends.at[stage, unit_index],
                recv_sem=recvs.at[stage, unit_index],
                device_id=(gx, to_y),
                device_id_type=MESH,
            ).start()

    def scatter_fields(u):
        parts = granules(UNITS[u])
        for i in range(N_GY):
            for g in range(parts):
                start = UNITS[u][1] + (i * parts + g) * GRANULE
                fields[u][i, g] = acc[start : start + GRANULE].astype(jnp.bfloat16)
        to_peers(fields[u], gathered[u], lambda device: device, 0, u)

    def frequency_slot(device):
        freq = rem(device, 2) * 8 + rem(div(device, 2), 2) * 4
        freq = freq + rem(div(device, 4), 2) * 2 + div(device, 8)
        return 8 - (freq - 8) * (2 * div(freq, 8) - 1)

    def transform(u):
        pltpu.make_async_copy(gathered[u], gathered[u], recvs.at[0, u]).wait()
        for g in range(granules(UNITS[u])):
            for half in range(LANES // 128):
                lanes = slice(128 * half, 128 * half + 128)
                values = [gathered[u][s, g, :, lanes].astype(jnp.float32) for s in range(N_GY)]
                for r, (re, im) in enumerate(real_transform(values)):
                    im = jnp.zeros_like(re) if im is None else im
                    partials[u][r, g, 0, :, lanes] = re.astype(jnp.bfloat16)
                    partials[u][r, g, 1, :, lanes] = im.astype(jnp.bfloat16)
        to_peers(partials[u], outs[u], frequency_slot, 1, u)

    def run(pair, low, rows, first, last, phases, arriving=False, between=None):
        def step(i, carry):
            if between is not None:

                @pl.when(i == between[0])
                def _():
                    transform(between[1])

            for phase in range(phases if arriving else 0):
                arrived = recv.at[pl.ds(0, N_GY)]
                sem = route_recv.at[i * phases + phase]
                pltpu.make_async_copy(arrived, arrived, sem).wait()
            deposit(pair, low, rows, i * phases, phases)
            return carry

        lax.fori_loop(first // phases, last // phases, step, 0)

    acc[...] = jnp.zeros_like(acc)
    run(0, 0, ROWS, 0, 4, 1, arriving=True)
    run(0, 0, HALF, 4, N_GX, 1, arriving=True)
    scatter_fields(0)
    run(0, HALF, HALF, 4, N_GX, 2)
    scatter_fields(1)
    for u in range(2, count):
        if u % 2 == 0:
            acc[...] = jnp.zeros_like(acc)
        run(*UNITS[u], 0, N_GX, 4, between=(1, 0) if u == 2 else None)
        scatter_fields(u)
        transform(u - 1)

    def finish(u):
        pltpu.make_async_copy(outs[u], outs[u], recvs.at[1, u]).wait()
        pair, low, rows = UNITS[u]
        unit_lines(UNITS[u], matrix, outs[u], staged, 2 * pair, low // CY)
        for half in range(2):
            at = (half, pl.ds(2 * pair, 2), pl.ds(low // CY, rows // CY))
            copy = pltpu.make_async_copy(staged.at[at], done_ref.at[at], done_sems.at[u, half])
            copy.start()
            moved.append(copy)

    moved = [matrix_load]
    own_load.wait()
    for u in range(count - 3):
        finish(u)
    transform(count - 1)
    finish(count - 3)
    finish(count - 2)
    for copy in moved:
        copy.wait()

    sent = send_ref.at[pl.ds(0, DEVICES - 1)]
    pltpu.make_async_copy(sent, sent, route_send).wait()
    for u in range(count):
        sent = fields[u].at[pl.ds(0, N_GY - 1)]
        pltpu.make_async_copy(sent, sent, sends.at[0, u]).wait()
        sent = outs[u].at[pl.ds(0, N_GY - 1)]
        pltpu.make_async_copy(sent, sent, sends.at[1, u]).wait()
    pltpu.make_async_copy(outs[-1], outs[-1], recvs.at[1, count - 1]).wait()


def lines_kernel(matrix, part, done_ref, out_ref, last, sems):
    pair, low, rows = UNITS[-1]
    copies = []
    for half in range(2):
        for u in range(len(UNITS) - 1):
            at = (half, pl.ds(2 * UNITS[u][0], 2), pl.ds(UNITS[u][1] // CY, UNITS[u][2] // CY))
            copies.append((done_ref.at[at], out_ref.at[at]))
    for i, (source, target) in enumerate(copies):
        pltpu.make_async_copy(source, target, sems.at[i]).start()
    unit_lines(UNITS[-1], matrix, part, last, 0, 0)
    for half in range(2):
        at = (half, pl.ds(2 * pair, 2), pl.ds(low // CY, rows // CY))
        copies.append((last.at[half], out_ref.at[at]))
        i = len(copies) - 1
        pltpu.make_async_copy(*copies[i], sems.at[i]).start()
    for i, (source, target) in enumerate(copies):
        pltpu.make_async_copy(source, target, sems.at[i]).wait()


def line_table():
    y = np.arange(CY)
    q = np.arange(CY)
    tables = []
    for freq in range(N_GY):
        phase = (q[:, None] * N_GY + freq) * y[None, :] % (CY * N_GY)
        angle = phase * (2.0 * np.pi / (CY * N_GY))
        cos, sin = np.cos(angle), np.sin(angle)
        sign = -1.0 if freq > N_GY // 2 else 1.0
        full = np.stack([np.stack([cos, sign * sin], 1), np.stack([-sin, sign * cos], 1)])
        full = full.reshape(2, CY, 2, CY // GRANULE, GRANULE).transpose(0, 1, 3, 2, 4)
        full = full.reshape(2 * CY, 2 * CY)
        high = full.astype(jnp.bfloat16)
        tables.append(np.stack([high, (full - high.astype(np.float64)).astype(jnp.bfloat16)]))
    return np.stack(tables)


def shards(table, offsets, weights, owners, cells):
    unit_shapes = [(N_GY, granules(unit), GRANULE, LANES) for unit in UNITS]
    half_shapes = [(9, granules(unit), 2, GRANULE, LANES) for unit in UNITS]
    out_shapes = [(N_GY, granules(unit), 2, GRANULE, LANES) for unit in UNITS]
    part, matrix, done = pl.pallas_call(
        exchange_kernel,
        out_shape=[
            jax.ShapeDtypeStruct(out_shapes[-1], jnp.bfloat16),
            jax.ShapeDtypeStruct((2, 2 * CY, 2 * CY), jnp.bfloat16),
            jax.ShapeDtypeStruct((2, 6, CX, CY, NZ), jnp.float32),
        ],
        in_specs=[HBM] * 5,
        out_specs=[ANY] * 3,
        scratch_shapes=[
            *[pltpu.VMEM(shape, jnp.bfloat16) for shape in out_shapes[:-1]],
            *[pltpu.VMEM(shape, jnp.bfloat16) for shape in unit_shapes],
            *[pltpu.VMEM(shape, jnp.bfloat16) for shape in unit_shapes],
            *[pltpu.VMEM(shape, jnp.bfloat16) for shape in half_shapes],
            pltpu.VMEM((1, NB), jnp.int32),
            pltpu.VMEM((NB, 3, BP), jnp.float32),
            pltpu.VMEM((NB, BP), jnp.float32),
            pltpu.VMEM((NB, BP), jnp.int32),
            pltpu.VMEM((DEVICES * CAP * 8, BP), jnp.float32),
            pltpu.VMEM((DEVICES, CAP, 8, BP), jnp.bfloat16),
            pltpu.VMEM((DEVICES, CAP, 8, BP), jnp.bfloat16),
            pltpu.VMEM((ROWS, LANES), jnp.float32),
            pltpu.VMEM((2, 2 * CY, 2 * CY), jnp.bfloat16),
            pltpu.VMEM((2, 6, CX, CY, NZ), jnp.float32),
            pltpu.SemaphoreType.DMA((6,)),
            pltpu.SemaphoreType.DMA,
            pltpu.SemaphoreType.DMA((N_GX,)),
            pltpu.SemaphoreType.DMA((2, len(UNITS))),
            pltpu.SemaphoreType.DMA((2, len(UNITS))),
            pltpu.SemaphoreType.DMA((len(UNITS) - 1, 2)),
        ],
        compiler_params=pltpu.CompilerParams(
            has_side_effects=True, collective_id=0, vmem_limit_bytes=48 << 20
        ),
        name="exchange",
    )(
        *[
            pltpu.with_memory_space_constraint(array, pltpu.HBM)
            for array in (
                owners.reshape(1, NB),
                jnp.transpose(offsets.reshape(3, NB, BP), (1, 0, 2)),
                weights.reshape(NB, BP),
                cells.reshape(NB, BP),
                table,
            )
        ]
    )
    return pl.pallas_call(
        lines_kernel,
        out_shape=jax.ShapeDtypeStruct((2, 6, CX, CY, NZ), jnp.float32),
        in_specs=[VMEM] * 3,
        out_specs=HBM,
        scratch_shapes=[
            pltpu.VMEM((2, 2, UNITS[-1][2] // CY, CY, NZ), jnp.float32),
            pltpu.SemaphoreType.DMA((2 * len(UNITS),)),
        ],
        compiler_params=pltpu.CompilerParams(vmem_limit_bytes=8 << 20),
        name="lines",
    )(matrix, part, done)


def solution(mesh):
    table = line_table()
    placed = (P(None, ("gx", "gy")), P(("gx", "gy")), P(("gx", "gy"), None), P(("gx", "gy")))
    mapped = jax.shard_map(
        shards,
        mesh=mesh,
        in_specs=(P(),) + placed,
        out_specs=P(None, None, "gx", "gy", None),
        check_vma=False,
    )
    return functools.partial(mapped, jnp.asarray(table))
```
